256 devices in a mesh: dp: 32 (over y, z_lo, x), fsdp: 8 (over z_hi, core).
Axes of the slice: x: 4, y: 4, z: 8 (z_hi: 4, z_lo: 2; z = z_hi * 2 + z_lo), core: 2. Of those that a mesh axis runs over, the one named last changes fastest.
Arguments:
- stretch_tokens: bfloat16 [32, 512, 2560], P('dp', 'fsdp'), may hold values from -6 to 6
- norm_gain: bfloat16 [2560], replicated, may hold values from 0.25 to 1.75
- w_query: bfloat16 [2560, 1280], P(('dp', 'fsdp')), may hold values from -0.25 to 0.25
- w_keyval: bfloat16 [2560, 640], P(('dp', 'fsdp')), may hold values from -0.25 to 0.25
- w_out: bfloat16 [2560, 1280], P(('dp', 'fsdp')), may hold values from -0.3125 to 0.3125
- cache_store: bfloat16 [32, 4096, 640], P(None, ('dp', 'fsdp'))
- cache_lengths: int32 [32], replicated, may hold values from 1 to 4096, as said below
- source_slot: int32 [32], replicated, may hold values from 0 to 31, each once
Outputs:
- update: bfloat16 [32, 512, 2560], P('dp', 'fsdp')
- new_keyval: bfloat16 [32, 512, 640], P('dp', 'fsdp')
The draws below stay inside these ranges and needn't reach their ends.
Inputs may be any that keep to these rules, and one draw needn't show every extreme that they name: `cache_lengths`: one request has exactly 4096 cached positions. `source_slot`: every request is served in exactly one slot.
All inputs are finite; a program needn't handle non-finite values.
Results may differ from the reference program's by a relative error of at most 0.015.
The reference program's roundings to bfloat16 on the way (of `normed`, `queries`, `weights` and `attended`) count: a program that leaves them out, or rounds other values in their place, can miss the bound.
Values may be sent and summed in bfloat16 or wider, within the bound.
A program may use at most 128 MiB of HBM per device.

```python
import jax
import jax.numpy as jnp
from jax import lax

D = 2560
HEAD_DIM = 80
HEADS = 16
KV_HEADS = 4
STRETCH = 512
CACHE_MAX = 4096
REQUESTS = 32
QW = 1280
KVW = 640


def draw_cache_store(key, part):
    base_key = jax.random.fold_in(key, 0)
    values = 2.0 * jax.random.truncated_normal(base_key, -4.0, 4.0, (REQUESTS, CACHE_MAX, KVW), jnp.float32)
    return values.astype(jnp.bfloat16)


def draw_cache_lengths(key, part):
    length_key, pick_key = jax.random.split(jax.random.fold_in(key, 7))
    lengths = jax.random.randint(length_key, (REQUESTS,), 1, CACHE_MAX + 1)
    chosen = jax.random.randint(pick_key, (), 0, REQUESTS)
    return jnp.where(jnp.arange(REQUESTS) == chosen, CACHE_MAX, lengths).astype(jnp.int32)


def block_scale(stream_key, extent, shards, smallest, largest):
    level, own = 1.0, jax.random.fold_in(stream_key, 6)
    for axis_at, blocks in shards:
        heights = jnp.exp(jax.random.uniform(jax.random.fold_in(own, axis_at), (blocks,), jnp.float32, smallest / len(shards), largest / len(shards)))
        level = level * jnp.repeat(heights, extent[axis_at] // blocks).reshape([-1 if axis == axis_at else 1 for axis in range(len(extent))])
    return level


def centred(key, shape, scale, reach, cuts=(), kind=jnp.bfloat16):
    values = jax.random.normal(key, shape, jnp.float32) * scale
    if len(cuts) > 0:
        values = block_scale(key, shape, cuts, -0.22, 0.18) * values
    return jnp.clip(values, min=-reach, max=reach).astype(kind)


def setup_inputs(seed: int = 0) -> dict:
    splits = jax.random.split(jax.random.key(seed), 9)
    return {
        "stretch_tokens": centred(splits[0], (REQUESTS, STRETCH, D), 1.0, 6.0, ((0, 32), (1, 8))),
        "norm_gain": jnp.clip(1.0 + 0.15 * jax.random.normal(splits[1], (D,), jnp.float32), 0.25, 1.75).astype(jnp.bfloat16),
        "w_query": centred(splits[2], (D, QW), (D // 4) ** -0.5, 0.25, ((0, 256),)),
        "w_keyval": centred(splits[3], (D, KVW), (D // 4) ** -0.5, 0.25, ((0, 256),)),
        "w_out": centred(splits[4], (D, QW), (QW // 4) ** -0.5, 0.3125, ((0, 256),)),
        "cache_store": draw_cache_store(jax.random.fold_in(splits[8], 71), 0),
        "cache_lengths": draw_cache_lengths(jax.random.fold_in(splits[8], 71), 0),
        "source_slot": jax.random.permutation(splits[7], REQUESTS).astype(jnp.int32),
    }


ROPE_BASE = 1000000.0
EPSILON = 1e-05
NEGATIVE = -1e+30

def rotate(vectors, positions):
    half = vectors.shape[-1] // 2
    frequency = ROPE_BASE ** (-(jnp.arange(half, dtype=jnp.float32) * 2.0) / vectors.shape[-1])
    angles = positions.astype(jnp.float32)[..., None, None] * frequency
    cosine = jnp.cos(angles)
    sine = jnp.sin(angles)
    first = vectors[..., :half]
    second = vectors[..., half:]
    return jnp.concatenate([first * cosine - second * sine, second * cosine + first * sine], axis=-1)

def reference(stretch_tokens, norm_gain, w_query, w_keyval, w_out, cache_store, cache_lengths, source_slot):
    group = HEADS // KV_HEADS
    tokens = stretch_tokens.astype(jnp.float32)
    squares = lax.optimization_barrier(jnp.mean(tokens * tokens, axis=-1, keepdims=True))
    normed = (tokens * lax.rsqrt(squares + EPSILON) * norm_gain.astype(jnp.float32)).astype(jnp.bfloat16)
    flat = normed.reshape(REQUESTS * STRETCH, D)
    raw_query = jnp.dot(flat, w_query, preferred_element_type=jnp.float32).reshape(REQUESTS, STRETCH, HEADS, HEAD_DIM)
    raw_keyval = jnp.dot(flat, w_keyval, preferred_element_type=jnp.float32).reshape(REQUESTS, STRETCH, 2, KV_HEADS, HEAD_DIM)
    slot_lengths = cache_lengths[source_slot].astype(jnp.int32)
    positions = slot_lengths[:, None] + jnp.arange(STRETCH, dtype=jnp.int32)[None, :]
    queries = rotate(raw_query, positions).astype(jnp.bfloat16)
    keys = rotate(raw_keyval[:, :, 0], positions)
    new_keyval = jnp.concatenate([keys.reshape(REQUESTS, STRETCH, KV_HEADS * HEAD_DIM), raw_keyval[:, :, 1].reshape(REQUESTS, STRETCH, KV_HEADS * HEAD_DIM)], axis=-1).astype(jnp.bfloat16)

    def attend(inputs):
        query, fresh, source, length = inputs
        stored = cache_store[source]
        every = jnp.concatenate([stored, fresh], axis=0)
        key_all = every[:, :KV_HEADS * HEAD_DIM].reshape(-1, KV_HEADS, HEAD_DIM).astype(jnp.float32)
        value_all = every[:, KV_HEADS * HEAD_DIM:].reshape(-1, KV_HEADS, HEAD_DIM).astype(jnp.float32)
        grouped = query.reshape(STRETCH, KV_HEADS, group, HEAD_DIM).astype(jnp.float32)
        scores = jnp.einsum('tkgd,nkd->kgtn', grouped, key_all) * HEAD_DIM ** (-0.5)
        index = jnp.arange(CACHE_MAX + STRETCH, dtype=jnp.int32)
        token = jnp.arange(STRETCH, dtype=jnp.int32)
        valid = jnp.where(index[None, :] < CACHE_MAX, index[None, :] < length, index[None, :] - CACHE_MAX <= token[:, None])
        scores = jnp.where(valid, scores, NEGATIVE)
        top = lax.optimization_barrier(jnp.max(scores, axis=-1, keepdims=True))
        weights = jnp.where(valid, jnp.exp(scores - top), 0.0).astype(jnp.bfloat16)
        total = lax.optimization_barrier(jnp.sum(weights.astype(jnp.float32), axis=-1))
        numer = jnp.einsum('kgtn,nkd->kgtd', weights.astype(jnp.float32), value_all)
        result = numer / total[..., None]
        return result.transpose(2, 0, 1, 3).reshape(STRETCH, HEADS * HEAD_DIM).astype(jnp.bfloat16)
    attended = lax.map(attend, (queries, new_keyval, source_slot, slot_lengths))
    update = jnp.dot(attended.reshape(REQUESTS * STRETCH, HEADS * HEAD_DIM), w_out.T, preferred_element_type=jnp.float32).astype(jnp.bfloat16)
    return (update.reshape(REQUESTS, STRETCH, D), new_keyval)
```

```python
import functools

import jax
import jax.numpy as jnp
from jax import lax
from jax.experimental import pallas as pl
from jax.experimental.pallas import tpu as pltpu
from jax.sharding import PartitionSpec as P

MESH = pl.DeviceIdType.MESH
BF16 = jnp.bfloat16
F32 = jnp.float32

HEAD_DIM = 80
HEADS = 16
KV_HEADS = 4
ROPE_BASE = 1000000.0
EPSILON = 1e-05
NEGATIVE = -1e30
LOG2E = 1.4426950408889634

NX, NY, NZL, NZH = 4, 4, 2, 4
DP, GROUP = 32, 8
TOK = 64
WIDTH = 2560
PAGE = 16
ROWS = 80

UNITS = ((0, 0, 1, 0), (0, 1, 1, 1), (1, 0, 3, 0), (1, 3, 2, 1))

S1 = 0
S2 = 8
TK = 10
CX = 20
RING = 28
PER_UNIT = 13
C1 = RING + PER_UNIT * len(UNITS)
NSEM = C1 + DP


def one_hot(rows, columns, test):
    r = lax.broadcasted_iota(jnp.int32, (rows, columns), 0)
    l = lax.broadcasted_iota(jnp.int32, (rows, columns), 1)
    return jnp.where(test(r, l), 1.0, 0.0).astype(BF16)


def exact_dot(a, b):
    return jnp.dot(a, b, preferred_element_type=F32)


def gather_kernel(
    tok, wp, cache, toks_all, w_qkv, w_out, kv, s1buf, blk, cbuf, pack, send, recv, local
):
    dp = lax.axis_index("dp")
    f = lax.axis_index("fsdp")
    y, rest = dp // 8, dp % 8
    zl, x = rest // 4, rest % 4
    zh, c = f // 2, f % 2

    def dp_of(yy, zz, xx):
        return (yy * 2 + zz) * 4 + xx

    barrier = pltpu.get_barrier_semaphore()

    def greet_group(d, carry):
        pl.semaphore_signal(
            barrier, inc=1, device_id=(dp, (f + d) % GROUP), device_id_type=MESH
        )
        return carry

    def greet_data(d, carry):
        pl.semaphore_signal(barrier, inc=1, device_id=((dp + d) % DP, f), device_id_type=MESH)
        return carry

    lax.fori_loop(1, GROUP, greet_group, 0)
    lax.fori_loop(1, DP, greet_data, 0)
    pl.semaphore_wait(barrier, GROUP - 1 + DP - 1)

    started = []

    def rcopy(src, dst, sem, dev):
        cp = pltpu.make_async_remote_copy(
            src_ref=src,
            dst_ref=dst,
            send_sem=send.at[sem],
            recv_sem=recv.at[sem],
            device_id=dev,
            device_id_type=MESH,
        )
        cp.start()
        started.append(cp)
        return cp

    nlocal = [0]

    def lcopy(src, dst):
        cp = pltpu.make_async_copy(src, dst, local.at[nlocal[0]])
        nlocal[0] += 1
        cp.start()
        return cp

    twin = (dp, zh * 2 + 1 - c)

    s1 = []
    for d in range(1, GROUP):
        g = (f + d) % GROUP
        s1.append(
            rcopy(
                wp.at[g],
                s1buf.at[:, pl.ds(pl.multiple_of(f * 16, 16), 16), :],
                S1 + d,
                (dp, g),
            )
        )
    zp, zm = (zh + 1) % NZH, (zh + NZH - 1) % NZH
    zo = (zh + 2) % NZH
    t0 = rcopy(tok, toks_all.at[f], TK + 0, (dp, zp * 2 + c))
    t1 = rcopy(tok, toks_all.at[f], TK + 1, (dp, zm * 2 + c))
    t4 = rcopy(tok, toks_all.at[f], TK + 4, twin)
    tl = lcopy(tok, toks_all.at[f])

    def page_copy(d):
        there = (dp + d) % DP
        return pltpu.make_async_remote_copy(
            src_ref=cache.at[there],
            dst_ref=cbuf.at[dp],
            send_sem=send.at[C1 + d],
            recv_sem=recv.at[C1 + d],
            device_id=(there, f),
            device_id_type=MESH,
        )

    def page_start(d, carry):
        page_copy(d).start()
        return carry

    lax.fori_loop(1, DP, page_start, 0)
    cbuf[dp] = cache[dp]

    s1buf[:, pl.ds(pl.multiple_of(f * 16, 16), 16), :] = wp[f]
    for cp in s1:
        cp.wait_recv()
    squeeze = one_hot(ROWS, 128, lambda r, l: l == 16 * (r // 10) + r % 10)
    for t in range(7):
        blk[t] = exact_dot(squeeze, s1buf[t]).astype(BF16)

    there = dp_of(y, 1 - zl, x)
    mine_q = w_qkv.at[c, :, y, zl, x]
    mine_o = w_out.at[c, :, y, zl, x]
    q2 = rcopy(blk.at[pl.ds(0, 2)], mine_q, S2 + 0, (there, f))
    lq = lcopy(blk.at[pl.ds(0, 2)], mine_q)
    o2 = rcopy(blk.at[pl.ds(2, 5)], mine_o, S2 + 1, (there, f))
    lo = lcopy(blk.at[pl.ds(2, 5)], mine_o)

    xp, xm, xo = (x + 1) % NX, (x + NX - 1) % NX, (x + 2) % NX
    yp, ym, yo = (y + 1) % NY, (y + NY - 1) % NY, (y + 2) % NY
    devices = {
        0: ((dp_of(y, zl, xp), f), (dp_of(y, zl, xm), f)),
        1: ((dp_of(yp, zl, x), f), (dp_of(ym, zl, x), f)),
    }
    along = {0: (x, xm, xp, xo), 1: (y, ym, yp, yo)}

    def near(unit, at, half=None):
        which, lo_, n, axis = unit
        arr = (w_qkv, w_out)[which]
        z = slice(None) if half is None else half
        if axis == 0:
            return arr.at[c, pl.ds(lo_, n), y, z, at]
        return arr.at[c, pl.ds(lo_, n), at, z, x]

    def far(unit, at, half=None):
        which, lo_, n, axis = unit
        arr = (w_qkv, w_out)[which]
        z = slice(None) if half is None else half
        if axis == 0:
            return arr.at[c, pl.ds(lo_, n), at, z]
        return arr.at[c, pl.ds(lo_, n), :, z, at]

    class Ring:
        def __init__(self, u, second):
            self.unit = UNITS[u]
            self.base = RING + PER_UNIT * u + (4 if second else 0)
            self.axis = self.unit[3] if not second else 1 - self.unit[3]
            self.part = far if second else near
            self.at, self.minus, self.plus, self.other = along[self.axis]

        def start(self):
            up, down = devices[self.axis]
            own = self.part(self.unit, self.at)
            self.a = rcopy(own, own, self.base + 0, up)
            self.b = rcopy(own, own, self.base + 1, down)

        def relay(self):
            up, down = devices[self.axis]
            self.a.wait_recv()
            piece = self.part(self.unit, self.minus, 0)
            self.c = rcopy(piece, piece, self.base + 2, up)
            self.b.wait_recv()
            piece = self.part(self.unit, self.plus, 1)
            self.d = rcopy(piece, piece, self.base + 3, down)

        def finish(self):
            self.c.wait_recv()
            self.d.wait_recv()

    firsts = [Ring(u, False) for u in range(4)]
    seconds = [Ring(u, True) for u in range(4)]
    hands = []

    def hand(u, k, ref):
        hands.append(rcopy(ref, ref, RING + PER_UNIT * u + 8 + k, twin))

    def hand_own(u):
        hand(u, 0, far(UNITS[u], seconds[u].at))

    def hand_next(u):
        s = seconds[u]
        hand(u, 1, far(UNITS[u], s.minus))
        hand(u, 2, far(UNITS[u], s.plus))

    def hand_last(u):
        s = seconds[u]
        hand(u, 3, far(UNITS[u], s.other, 0))
        hand(u, 4, far(UNITS[u], s.other, 1))

    q2.wait_recv()
    lq.wait()
    firsts[0].start()
    firsts[1].start()
    o2.wait_recv()
    lo.wait()
    firsts[2].start()
    firsts[3].start()
    firsts[0].relay()
    firsts[1].relay()
    for u in (0, 1):
        firsts[u].finish()
        seconds[u].start()
        hand_own(u)
    firsts[2].relay()
    firsts[3].relay()
    for u in (2, 3):
        firsts[u].finish()
        seconds[u].start()
        hand_own(u)

    t0.wait_recv()
    ref = toks_all.at[zm * 2 + c]
    t2 = rcopy(
        toks_all.at[zm * 2 + c, pl.ds(0, 32)],
        toks_all.at[zm * 2 + c, pl.ds(0, 32)],
        TK + 2,
        (dp, zp * 2 + c),
    )
    t5 = rcopy(ref, ref, TK + 5, twin)
    t1.wait_recv()
    ref = toks_all.at[zp * 2 + c]
    t3 = rcopy(
        toks_all.at[zp * 2 + c, pl.ds(32, 32)],
        toks_all.at[zp * 2 + c, pl.ds(32, 32)],
        TK + 3,
        (dp, zm * 2 + c),
    )
    t6 = rcopy(ref, ref, TK + 6, twin)

    def page_wait(d, carry):
        page_copy(d).wait_recv()
        return carry

    lax.fori_loop(1, DP, page_wait, 0)
    pages = cbuf[...].reshape(DP * PAGE, 2 * KV_HEADS * HEAD_DIM)
    for k in range(KV_HEADS):

        def pick(r, l, k=k):
            value = KV_HEADS * HEAD_DIM + HEAD_DIM * k
            key = (l < 80) & (r == HEAD_DIM * k + l)
            front = (l >= 80) & (l < 128) & (r == value + l - 80)
            back = (l >= 128) & (r == value + 48 + l % 32)
            return key | front | back

        both = exact_dot(pages, one_hot(640, 256, pick))
        pack[k, pl.ds(0, 512), :] = both[:, :128].astype(BF16)
        lane = lax.broadcasted_iota(jnp.int32, (128, 128), 1) // 32
        tail = jnp.zeros((128, 128), F32)
        for g in range(4):
            tail = jnp.where(lane == g, both[128 * g : 128 * g + 128, 128:], tail)
        pack[k, pl.ds(512, 128), :] = tail.astype(BF16)
    heads = []
    for d in range(1, NZH):
        g = (zh + d) % NZH
        heads.append(rcopy(pack.at[g], kv.at[c, zh], CX + d, (dp, g * 2 + c)))
    hl = lcopy(pack.at[zh], kv.at[c, zh])
    hands.append(rcopy(pack.at[zh], kv.at[c, zh], CX + 4, twin))

    for u in (0, 1):
        seconds[u].relay()
        hand_next(u)
    for u in (2, 3):
        seconds[u].relay()
        hand_next(u)
    t2.wait_recv()
    ref = toks_all.at[zo * 2 + c, pl.ds(0, 32)]
    t7 = rcopy(ref, ref, TK + 7, twin)
    t3.wait_recv()
    ref = toks_all.at[zo * 2 + c, pl.ds(32, 32)]
    t8 = rcopy(ref, ref, TK + 8, twin)
    for u in (0, 1):
        seconds[u].finish()
        hand_last(u)
    for d in range(1, NZH):
        heads[d - 1].wait_recv()
        ref = kv.at[c, (zh + NZH - d) % NZH]
        hands.append(rcopy(ref, ref, CX + 4 + d, twin))
    for u in (2, 3):
        seconds[u].finish()
        hand_last(u)

    for cp in (t4, t5, t6, t7, t8, *hands):
        cp.wait_recv()
    for cp in started:
        cp.wait_send()

    def page_sent(d, carry):
        page_copy(d).wait_send()
        return carry

    lax.fori_loop(1, DP, page_sent, 0)
    tl.wait()
    hl.wait()


def gather_all(tok, wp, cache):
    vmem = pl.BlockSpec(memory_space=pltpu.VMEM)
    hbm = pl.BlockSpec(memory_space=pl.ANY)
    return pl.pallas_call(
        gather_kernel,
        out_shape=(
            jax.ShapeDtypeStruct((GROUP, TOK, WIDTH), BF16),
            jax.ShapeDtypeStruct((2, 2, NY, NZL, NX, ROWS, 128), BF16),
            jax.ShapeDtypeStruct((2, 5, NY, NZL, NX, ROWS, 128), BF16),
            jax.ShapeDtypeStruct((2, NZH, 640, 128), BF16),
        ),
        in_specs=[vmem, vmem, vmem],
        out_specs=(hbm, hbm, hbm, hbm),
        scratch_shapes=[
            pltpu.VMEM((7, 128, 128), BF16),
            pltpu.VMEM((7, ROWS, 128), BF16),
            pltpu.VMEM((DP, PAGE, 640), BF16),
            pltpu.VMEM((KV_HEADS, 640, 128), BF16),
            pltpu.SemaphoreType.DMA((NSEM,)),
            pltpu.SemaphoreType.DMA((NSEM,)),
            pltpu.SemaphoreType.DMA((8,)),
        ],
        compiler_params=pltpu.CompilerParams(collective_id=0, has_side_effects=True),
        name="gather_all",
    )(tok, wp, cache)


def attend_kernel(meta, x_ref, w_ref, kv_ref, cos_ref, sin_ref, out_ref, roped, kmat, vmat, qmat):
    c, length = meta[0], meta[1]
    x = x_ref[...].reshape(GROUP * TOK, WIDTH)
    lane = lax.broadcasted_iota(jnp.int32, (GROUP * TOK, 256), 1)
    early = lane % HEAD_DIM < HEAD_DIM // 2
    for half in range(2):
        w = jnp.concatenate([w_ref[half, 0], w_ref[half, 1]], axis=1)
        raw = exact_dot(x, w)
        turned = jnp.where(early, pltpu.roll(raw, 216, 1), pltpu.roll(raw, 40, 1))
        new = raw * cos_ref[...] + turned * sin_ref[...]
        if half == 1:
            new = jnp.where(lane < 160, new, raw)
        roped[half] = new.astype(BF16).reshape(NZH, 2, TOK, 256)
    row = lax.broadcasted_iota(jnp.int32, (512, 128), 0)
    lane = lax.broadcasted_iota(jnp.int32, (512, 128), 1)
    for cs in range(2):
        for zs in range(NZH):
            base = (cs * NZH + zs) * 512
            a = kv_ref[cs, zs, pl.ds(0, 512), :]
            position = (row // 16) * 128 + zs * 32 + cs * 16 + row % 16
            bias = jnp.where((lane == 80) & (position >= length), NEGATIVE, 0.0)
            kmat[pl.ds(base, 512), :] = jnp.where(lane < 80, a.astype(F32), bias).astype(BF16)
            vmat[pl.ds(base, 512), pl.ds(0, 128)] = a
            tail = kv_ref[cs, zs, pl.ds(512, 128), :]
            ones = jnp.where(lane[:128] == 32, 1.0, 0.0)
            for g in range(4):
                pick = one_hot(128, 128, lambda r, l: (l < 32) & (r == 32 * g + l))
                vmat[pl.ds(base + 128 * g, 128), pl.ds(128, 128)] = (
                    exact_dot(tail, pick) + ones
                ).astype(BF16)
    first = roped[0].reshape(512, 256)
    second = roped[1].reshape(512, 256)
    to_key = one_hot(256, 128, lambda r, l: (l < 80) & (r == 160 + l))
    kmat[pl.ds(4096, 512), :] = exact_dot(first, to_key).astype(BF16)
    to_value = one_hot(256, 256, lambda r, l: (l >= 80) & (l < 160) & (r == 80 + l))
    lane = lax.broadcasted_iota(jnp.int32, (512, 256), 1)
    ones = jnp.where(lane == 160, 1.0, 0.0)
    vmat[pl.ds(4096, 512), :] = (exact_dot(second, to_value) + ones).astype(BF16)

    lane = lax.broadcasted_iota(jnp.int32, (256, 128), 1)
    ones = jnp.where(lane == 80, 1.0, 0.0)
    own = [roped[half, :, c].reshape(256, 256) for half in range(2)]
    for h in range(4):
        off = HEAD_DIM * (h % 2)
        to_head = one_hot(256, 128, lambda r, l: (l < 80) & (r == off + l))
        qmat[h] = (exact_dot(own[h // 2], to_head) + ones).astype(BF16)

    row = lax.broadcasted_iota(jnp.int32, (256, 512), 0)
    col = lax.broadcasted_iota(jnp.int32, (256, 512), 1)
    token = (row // 64) * 128 + c * 64 + row % 64
    causal = jnp.where(col <= token, 0.0, NEGATIVE)
    scale = LOG2E * HEAD_DIM ** (-0.5)
    nt = (((1,), (1,)), ((), ()))

    out = exact_dot(
        own[0], one_hot(256, 512, lambda r, l: (l >= 320) & (l < 400) & (r == l - 160))
    ) + exact_dot(
        own[1], one_hot(256, 512, lambda r, l: (l >= 400) & (l < 480) & (r == l - 240))
    )
    for h in range(4):
        q = qmat[h]
        s = lax.dot_general(q, kmat[pl.ds(4096, 512), :], nt, preferred_element_type=F32) + causal
        top = jnp.max(s, axis=1, keepdims=True)
        p = jnp.exp2((s - top) * scale).astype(BF16)
        acc = exact_dot(p, vmat[pl.ds(4096, 512), :])
        for j in range(4):
            s = lax.dot_general(
                q, kmat[pl.ds(1024 * j, 1024), :], nt, preferred_element_type=F32
            )
            new_top = jnp.maximum(top, jnp.max(s, axis=1, keepdims=True))
            p = jnp.exp2((s - new_top) * scale).astype(BF16)
            acc = acc * jnp.exp2((top - new_top) * scale) + exact_dot(
                p, vmat[pl.ds(1024 * j, 1024), :]
            )
            top = new_top
        att = (acc / acc[:, 160:161]).astype(BF16)
        out = out + exact_dot(
            att,
            one_hot(256, 512, lambda r, l: (r >= 80) & (r < 160) & (l == 80 * h + r - 80)),
        )
    out_ref[...] = out.astype(BF16).reshape(NZH, TOK, 512)


def attend(meta, x, w, kv, cosine, sine):
    vmem = pl.BlockSpec(memory_space=pltpu.VMEM)
    return pl.pallas_call(
        attend_kernel,
        out_shape=jax.ShapeDtypeStruct((NZH, TOK, 512), BF16),
        in_specs=[pl.BlockSpec(memory_space=pltpu.SMEM), vmem, vmem, vmem, vmem, vmem],
        out_specs=vmem,
        scratch_shapes=[
            pltpu.VMEM((2, NZH, 2, TOK, 256), BF16),
            pltpu.VMEM((4608, 128), BF16),
            pltpu.VMEM((4608, 256), BF16),
            pltpu.VMEM((4, 256, 128), BF16),
        ],
        compiler_params=pltpu.CompilerParams(vmem_limit_bytes=60 * 1024 * 1024),
        name="attend",
    )(meta, x, w, kv, cosine, sine)


def project_kernel(msg, w_hbm, upd_ref, keyval_ref, rbuf, w, send, recv, local):
    dp = lax.axis_index("dp")
    f = lax.axis_index("fsdp")
    zh, c = f // 2, f % 2
    load = pltpu.make_async_copy(w_hbm, w, local.at[0])
    load.start()
    barrier = pltpu.get_barrier_semaphore()
    for d in range(1, NZH):
        g = (zh + d) % NZH
        pl.semaphore_signal(barrier, inc=1, device_id=(dp, g * 2 + c), device_id_type=MESH)
    pl.semaphore_wait(barrier, NZH - 1)
    copies = []
    for d in range(1, NZH):
        g = (zh + d) % NZH
        cp = pltpu.make_async_remote_copy(
            src_ref=msg.at[g],
            dst_ref=rbuf.at[zh],
            send_sem=send.at[d],
            recv_sem=recv.at[d],
            device_id=(dp, g * 2 + c),
            device_id_type=MESH,
        )
        cp.start()
        copies.append(cp)
    rbuf[zh] = msg[zh]
    keyval = jnp.zeros((TOK, 640), F32)
    load.wait()
    for cp in copies:
        cp.wait_recv()
    lane = lax.broadcasted_iota(jnp.int32, (TOK, 128), 1)
    attended = []
    for pair in range(2):
        a = rbuf[2 * pair].astype(F32)
        b = pltpu.roll(rbuf[2 * pair + 1].astype(F32)[:, :384], 64, 1)
        attended += [
            a[:, 0:256],
            jnp.concatenate(
                [jnp.where(lane < 64, a[:, 256:384], b[:, 0:128]), b[:, 128:256]], axis=1
            ),
            b[:, 256:384],
        ]
    for k in range(KV_HEADS):

        def place(r, l, k=k):
            key = (r >= 64) & (r < 144) & (l == 80 * k + r - 64)
            value = (r >= 144) & (r < 224) & (l == 320 + 80 * k + r - 144)
            return key | value

        keyval = keyval + exact_dot(rbuf[k][:, 256:512], one_hot(256, 640, place))
    keyval_ref[...] = keyval.astype(BF16)
    tiles = [t.astype(BF16) for t in attended]
    nt = (((1,), (1,)), ((), ()))
    spans = ((0, 2), (2, 2), (4, 1), (5, 2), (7, 2), (9, 1))
    for n in range(4):
        rows = pl.ds(640 * n, 640)
        total = jnp.zeros((TOK, 640), F32)
        for t, (lo, count) in zip(tiles, spans):
            parts = [w[(lo + i) // 5, (lo + i) % 5, rows, :] for i in range(count)]
            rhs = parts[0] if count == 1 else jnp.concatenate(parts, axis=1)
            total = total + lax.dot_general(t, rhs, nt, preferred_element_type=F32)
        upd_ref[:, 640 * n : 640 * n + 640] = total.astype(BF16)
    for cp in copies:
        cp.wait_send()


def project(msg, w):
    vmem = pl.BlockSpec(memory_space=pltpu.VMEM)
    return pl.pallas_call(
        project_kernel,
        out_shape=(
            jax.ShapeDtypeStruct((TOK, WIDTH), BF16),
            jax.ShapeDtypeStruct((TOK, 640), BF16),
        ),
        in_specs=[vmem, pl.BlockSpec(memory_space=pl.ANY)],
        out_specs=(vmem, vmem),
        scratch_shapes=[
            pltpu.VMEM((NZH, TOK, 512), BF16),
            pltpu.VMEM((2, 5, WIDTH, 128), BF16),
            pltpu.SemaphoreType.DMA((4,)),
            pltpu.SemaphoreType.DMA((4,)),
            pltpu.SemaphoreType.DMA((1,)),
        ],
        compiler_params=pltpu.CompilerParams(
            collective_id=1, has_side_effects=True, vmem_limit_bytes=40 * 1024 * 1024
        ),
        name="project",
    )(msg, w)


def pieces(w_query, w_keyval, w_out):
    rows = w_query.shape[0]
    q = w_query.reshape(rows, KV_HEADS, 2, 160)
    kv = w_keyval.reshape(rows, 2, KV_HEADS, HEAD_DIM).transpose(0, 2, 1, 3)
    qkv = jnp.concatenate([q, kv, jnp.zeros((rows, KV_HEADS, 2, 16), BF16)], axis=-1)
    qkv = qkv.reshape(rows, GROUP, 2, 128).transpose(1, 2, 0, 3)
    o = w_out.reshape(rows, 2, 5, 128).transpose(1, 2, 0, 3)
    o = jnp.broadcast_to(o[None], (KV_HEADS, 2, 5, rows, 128)).reshape(GROUP, 5, rows, 128)
    both = jnp.concatenate([qkv, o], axis=1)
    return jnp.pad(both, ((0, 0), (0, 0), (0, 16 - rows), (0, 0)))


def on_device(
    stretch_tokens, norm_gain, w_query, w_keyval, w_out, cache_store, cache_lengths, source_slot
):
    dp = lax.axis_index("dp")
    f = lax.axis_index("fsdp")
    tokens = stretch_tokens[0].astype(F32)
    squares = jnp.mean(tokens * tokens, axis=-1, keepdims=True)
    normed = (tokens * lax.rsqrt(squares + EPSILON) * norm_gain.astype(F32)).astype(BF16)
    length = cache_lengths[source_slot[dp]]
    ordered = cache_store[source_slot]
    toks_all, w_qkv, w_o, kv = gather_all(normed, pieces(w_query, w_keyval, w_out), ordered)

    half = HEAD_DIM // 2
    frequency = ROPE_BASE ** (-(jnp.arange(half, dtype=F32) * 2.0) / HEAD_DIM)
    positions = length + jnp.arange(GROUP * TOK, dtype=jnp.int32)
    angles = positions.astype(F32)[:, None] * frequency
    cosine, sine = jnp.cos(angles), jnp.sin(angles)
    pad = jnp.zeros((GROUP * TOK, 16), F32)
    cosine = jnp.concatenate([cosine] * 6 + [pad], axis=1)
    sine = jnp.concatenate([-sine, sine] * 3 + [pad], axis=1)

    meta = jnp.stack([f % 2, length]).astype(jnp.int32)
    msg = attend(meta, toks_all, w_qkv.reshape(2, 2, WIDTH, 128), kv, cosine, sine)
    update, new_keyval = project(msg, w_o.reshape(2, 5, WIDTH, 128))
    return (update[None], new_keyval[None])


def solution(mesh):
    in_specs = (
        P("dp", "fsdp", None),
        P(),
        P(("dp", "fsdp"), None),
        P(("dp", "fsdp"), None),
        P(("dp", "fsdp"), None),
        P(None, ("dp", "fsdp"), None),
        P(),
        P(),
    )
    out_specs = (P("dp", "fsdp", None), P("dp", "fsdp", None))
    return jax.shard_map(
        on_device, mesh=mesh, in_specs=in_specs, out_specs=out_specs, check_vma=False
    )
```

```python
import functools

import jax
import jax.numpy as jnp
from jax import lax
from jax.experimental import pallas as pl
from jax.experimental.pallas import tpu as pltpu
from jax.sharding import PartitionSpec as P

MESH = pl.DeviceIdType.MESH
BF16 = jnp.bfloat16
F32 = jnp.float32

HEAD_DIM = 80
HEADS = 16
KV_HEADS = 4
ROPE_BASE = 1000000.0
EPSILON = 1e-05
NEGATIVE = -1e30
LOG2E = 1.4426950408889634

NX, NY, NZL, NZH = 4, 4, 2, 4
DP, GROUP = 32, 8
TOK = 64
WIDTH = 2560
PAGE = 16
ROWS = 80
S1ROWS = 10

UNITS = ((0, 0, 1, 0), (0, 1, 1, 1), (1, 0, 3, 0), (1, 3, 2, 1))

S1 = 0
S2 = 8
TK = 10
CX = 20
RING = 36
PER_UNIT = 13
C1 = RING + PER_UNIT * len(UNITS)
NSEM = C1 + DP


def one_hot(rows, columns, test):
    r = lax.broadcasted_iota(jnp.int32, (rows, columns), 0)
    l = lax.broadcasted_iota(jnp.int32, (rows, columns), 1)
    return jnp.where(test(r, l), 1.0, 0.0).astype(BF16)


def exact_dot(a, b):
    return jnp.dot(a, b, preferred_element_type=F32)


def gather_kernel(
    slots, raw, gain, wq_ref, wkv_ref, wo_ref, cache_ref, toks_all, w_qkv, w_out, kv,
    tok, stage, wp, cache, s1buf, blk, cbuf, pack, relay, send, recv, local
):
    dp = lax.axis_index("dp")
    f = lax.axis_index("fsdp")
    y, rest = dp // 8, dp % 8
    zl, x = rest // 4, rest % 4
    zh, c = f // 2, f % 2

    def dp_of(yy, zz, xx):
        return (yy * 2 + zz) * 4 + xx

    s1buf[...] = jnp.zeros_like(s1buf)
    barrier = pltpu.get_barrier_semaphore()

    def greet_group(d, carry):
        pl.semaphore_signal(
            barrier, inc=1, device_id=(dp, (f + d) % GROUP), device_id_type=MESH
        )
        return carry

    def greet_data(d, carry):
        pl.semaphore_signal(barrier, inc=1, device_id=((dp + d) % DP, f), device_id_type=MESH)
        return carry

    lax.fori_loop(1, GROUP, greet_group, 0)
    lax.fori_loop(1, DP, greet_data, 0)

    tokens = raw[...].astype(F32)
    squares = jnp.mean(tokens * tokens, axis=-1, keepdims=True)
    tok[...] = (tokens * lax.rsqrt(squares + EPSILON) * gain[...].astype(F32)).astype(BF16)
    stage[...] = jnp.zeros_like(stage)
    stage[pl.ds(0, 10), pl.ds(0, 1280)] = wq_ref[...].astype(F32)
    stage[pl.ds(0, 10), pl.ds(1280, 640)] = wkv_ref[...].astype(F32)
    stage[pl.ds(0, 10), pl.ds(1920, 1280)] = wo_ref[...].astype(F32)
    lane = lax.broadcasted_iota(jnp.int32, (16, 256), 1)
    for g in range(GROUP):
        k, half = g // 2, g % 2
        start = 160 * g
        base = start // 128 * 128
        q = stage[:, base : base + 256]
        if start > base:
            q = pltpu.roll(q, 256 - (start - base), 1)
        start = 320 * half + HEAD_DIM * k
        base = min(start // 128 * 128, 384)
        rest_ = stage[:, 1280 + base : 1536 + base]
        shift = (160 - (start - base)) % 256
        if shift:
            rest_ = pltpu.roll(rest_, shift, 1)
        both = jnp.where(lane < 160, q, jnp.where(lane < 240, rest_, 0.0)).astype(BF16)
        wp[g, 0] = both[:, :128]
        wp[g, 1] = both[:, 128:]
        for t in range(5):
            at = 1920 + 640 * half + 128 * t
            wp[g, 2 + t] = stage[:, at : at + 128].astype(BF16)
    for slot in range(DP):
        cache[slot] = cache_ref[slots[slot]]
    pl.semaphore_wait(barrier, GROUP - 1 + DP - 1)

    started = []

    def rcopy(src, dst, sem, dev):
        cp = pltpu.make_async_remote_copy(
            src_ref=src,
            dst_ref=dst,
            send_sem=send.at[sem],
            recv_sem=recv.at[sem],
            device_id=dev,
            device_id_type=MESH,
        )
        cp.start()
        started.append(cp)
        return cp

    nlocal = [0]

    def lcopy(src, dst):
        cp = pltpu.make_async_copy(src, dst, local.at[nlocal[0]])
        nlocal[0] += 1
        cp.start()
        return cp

    twin = (dp, zh * 2 + 1 - c)

    s1 = []
    for d in range(1, GROUP):
        g = (f + d) % GROUP
        s1.append(
            rcopy(
                wp.at[g, :, pl.ds(0, S1ROWS), :],
                s1buf.at[:, pl.ds(pl.multiple_of(f * 16, 16), S1ROWS), :],
                S1 + d,
                (dp, g),
            )
        )
    zp, zm = (zh + 1) % NZH, (zh + NZH - 1) % NZH
    zo = (zh + 2) % NZH
    t0 = rcopy(tok, toks_all.at[f], TK + 0, (dp, zp * 2 + c))
    t1 = rcopy(tok, toks_all.at[f], TK + 1, (dp, zm * 2 + c))
    t4 = rcopy(tok, toks_all.at[f], TK + 4, twin)
    tl = lcopy(tok, toks_all.at[f])

    def page_copy(d):
        there = (dp + d) % DP
        return pltpu.make_async_remote_copy(
            src_ref=cache.at[there],
            dst_ref=cbuf.at[dp],
            send_sem=send.at[C1 + d],
            recv_sem=recv.at[C1 + d],
            device_id=(there, f),
            device_id_type=MESH,
        )

    def page_start(d, carry):
        page_copy(d).start()
        return carry

    lax.fori_loop(1, DP, page_start, 0)
    cbuf[dp] = cache[dp]

    s1buf[:, pl.ds(pl.multiple_of(f * 16, 16), 16), :] = wp[f]
    for cp in s1:
        cp.wait_recv()
    squeeze = one_hot(ROWS, 128, lambda r, l: l == 16 * (r // 10) + r % 10)
    for t in range(7):
        blk[t] = exact_dot(squeeze, s1buf[t]).astype(BF16)

    there = dp_of(y, 1 - zl, x)
    mine_q = w_qkv.at[c, :, y, zl, x]
    mine_o = w_out.at[c, :, y, zl, x]
    q2 = rcopy(blk.at[pl.ds(0, 2)], mine_q, S2 + 0, (there, f))
    lq = lcopy(blk.at[pl.ds(0, 2)], mine_q)
    o2 = rcopy(blk.at[pl.ds(2, 5)], mine_o, S2 + 1, (there, f))
    lo = lcopy(blk.at[pl.ds(2, 5)], mine_o)

    xp, xm, xo = (x + 1) % NX, (x + NX - 1) % NX, (x + 2) % NX
    yp, ym, yo = (y + 1) % NY, (y + NY - 1) % NY, (y + 2) % NY
    devices = {
        0: ((dp_of(y, zl, xp), f), (dp_of(y, zl, xm), f)),
        1: ((dp_of(yp, zl, x), f), (dp_of(ym, zl, x), f)),
    }
    along = {0: (x, xm, xp, xo), 1: (y, ym, yp, yo)}

    def near(unit, at, half=None):
        which, lo_, n, axis = unit
        arr = (w_qkv, w_out)[which]
        z = slice(None) if half is None else half
        if axis == 0:
            return arr.at[c, pl.ds(lo_, n), y, z, at]
        return arr.at[c, pl.ds(lo_, n), at, z, x]

    def far(unit, at, half=None):
        which, lo_, n, axis = unit
        arr = (w_qkv, w_out)[which]
        z = slice(None) if half is None else half
        if axis == 0:
            return arr.at[c, pl.ds(lo_, n), at, z]
        return arr.at[c, pl.ds(lo_, n), :, z, at]

    class Ring:
        def __init__(self, u, second):
            self.unit = UNITS[u]
            self.base = RING + PER_UNIT * u + (4 if second else 0)
            self.axis = self.unit[3] if not second else 1 - self.unit[3]
            self.part = far if second else near
            self.at, self.minus, self.plus, self.other = along[self.axis]

        def start(self):
            up, down = devices[self.axis]
            own = self.part(self.unit, self.at)
            self.a = rcopy(own, own, self.base + 0, up)
            self.b = rcopy(own, own, self.base + 1, down)

        def relay(self):
            up, down = devices[self.axis]
            self.a.wait_recv()
            piece = self.part(self.unit, self.minus, 0)
            self.c = rcopy(piece, piece, self.base + 2, up)
            self.b.wait_recv()
            piece = self.part(self.unit, self.plus, 1)
            self.d = rcopy(piece, piece, self.base + 3, down)

        def finish(self):
            self.c.wait_recv()
            self.d.wait_recv()

    firsts = [Ring(u, False) for u in range(4)]
    seconds = [Ring(u, True) for u in range(4)]
    hands = []

    def hand(u, k, ref):
        hands.append(rcopy(ref, ref, RING + PER_UNIT * u + 8 + k, twin))

    def hand_own(u):
        hand(u, 0, far(UNITS[u], seconds[u].at))

    def hand_next(u):
        s = seconds[u]
        hand(u, 1, far(UNITS[u], s.minus))
        hand(u, 2, far(UNITS[u], s.plus))

    def hand_last(u):
        s = seconds[u]
        hand(u, 3, far(UNITS[u], s.other, 0))
        hand(u, 4, far(UNITS[u], s.other, 1))

    q2.wait_recv()
    lq.wait()
    firsts[0].start()
    firsts[1].start()
    o2.wait_recv()
    lo.wait()
    firsts[2].start()
    firsts[3].start()
    firsts[0].relay()
    firsts[1].relay()
    for u in (0, 1):
        firsts[u].finish()
        seconds[u].start()
        hand_own(u)
    firsts[2].relay()
    firsts[3].relay()
    for u in (2, 3):
        firsts[u].finish()
        seconds[u].start()
        hand_own(u)

    t0.wait_recv()
    ref = toks_all.at[zm * 2 + c]
    t2 = rcopy(
        toks_all.at[zm * 2 + c, pl.ds(0, 32)],
        toks_all.at[zm * 2 + c, pl.ds(0, 32)],
        TK + 2,
        (dp, zp * 2 + c),
    )
    t5 = rcopy(ref, ref, TK + 5, twin)
    t1.wait_recv()
    ref = toks_all.at[zp * 2 + c]
    t3 = rcopy(
        toks_all.at[zp * 2 + c, pl.ds(32, 32)],
        toks_all.at[zp * 2 + c, pl.ds(32, 32)],
        TK + 3,
        (dp, zm * 2 + c),
    )
    t6 = rcopy(ref, ref, TK + 6, twin)

    def page_wait(d, carry):
        page_copy(d).wait_recv()
        return carry

    lax.fori_loop(1, DP, page_wait, 0)
    pages = cbuf[...].reshape(DP * PAGE, 2 * KV_HEADS * HEAD_DIM)
    for k in range(KV_HEADS):

        def pick(r, l, k=k):
            value = KV_HEADS * HEAD_DIM + HEAD_DIM * k
            key = (l < 80) & (r == HEAD_DIM * k + l)
            front = (l >= 80) & (l < 128) & (r == value + l - 80)
            back = (l >= 128) & (r == value + 48 + l % 32)
            return key | front | back

        both = exact_dot(pages, one_hot(640, 256, pick))
        pack[k, pl.ds(0, 512), :] = both[:, :128].astype(BF16)
        lane = lax.broadcasted_iota(jnp.int32, (128, 128), 1) // 32
        tail = jnp.zeros((128, 128), F32)
        for g in range(4):
            tail = jnp.where(lane == g, both[128 * g : 128 * g + 128, 128:], tail)
        pack[k, pl.ds(512, 128), :] = tail.astype(BF16)
    up, down = (dp, zp * 2 + c), (dp, zm * 2 + c)
    h0 = rcopy(pack.at[zp], kv.at[c, zh], CX + 0, up)
    h1 = rcopy(pack.at[zm], kv.at[c, zh], CX + 1, down)
    h2 = rcopy(pack.at[zo, pl.ds(0, 320)], relay.at[0], CX + 2, up)
    h3 = rcopy(pack.at[zo, pl.ds(320, 320)], relay.at[1], CX + 3, down)
    hl = lcopy(pack.at[zh], kv.at[c, zh])
    hands.append(rcopy(pack.at[zh], kv.at[c, zh], CX + 6, twin))

    for u in (0, 1):
        seconds[u].relay()
        hand_next(u)
    h2.wait_recv()
    h4 = rcopy(relay.at[0], kv.at[c, zm, pl.ds(0, 320)], CX + 4, up)
    h3.wait_recv()
    h5 = rcopy(relay.at[1], kv.at[c, zp, pl.ds(320, 320)], CX + 5, down)
    for u in (2, 3):
        seconds[u].relay()
        hand_next(u)
    t2.wait_recv()
    ref = toks_all.at[zo * 2 + c, pl.ds(0, 32)]
    t7 = rcopy(ref, ref, TK + 7, twin)
    t3.wait_recv()
    ref = toks_all.at[zo * 2 + c, pl.ds(32, 32)]
    t8 = rcopy(ref, ref, TK + 8, twin)
    for u in (0, 1):
        seconds[u].finish()
        hand_last(u)
    h0.wait_recv()
    ref = kv.at[c, zm]
    hands.append(rcopy(ref, ref, CX + 7, twin))
    h1.wait_recv()
    ref = kv.at[c, zp]
    hands.append(rcopy(ref, ref, CX + 8, twin))
    h4.wait_recv()
    ref = kv.at[c, zo, pl.ds(0, 320)]
    hands.append(rcopy(ref, ref, CX + 9, twin))
    h5.wait_recv()
    ref = kv.at[c, zo, pl.ds(320, 320)]
    hands.append(rcopy(ref, ref, CX + 10, twin))
    for u in (2, 3):
        seconds[u].finish()
        hand_last(u)

    for cp in (t4, t5, t6, t7, t8, *hands):
        cp.wait_recv()
    for cp in started:
        cp.wait_send()

    def page_sent(d, carry):
        page_copy(d).wait_send()
        return carry

    lax.fori_loop(1, DP, page_sent, 0)
    tl.wait()
    hl.wait()


def gather_all(slots, raw, gain, w_query, w_keyval, w_out, cache):
    vmem = pl.BlockSpec(memory_space=pltpu.VMEM)
    hbm = pl.BlockSpec(memory_space=pl.ANY)
    return pl.pallas_call(
        gather_kernel,
        out_shape=(
            jax.ShapeDtypeStruct((GROUP, TOK, WIDTH), BF16),
            jax.ShapeDtypeStruct((2, 2, NY, NZL, NX, ROWS, 128), BF16),
            jax.ShapeDtypeStruct((2, 5, NY, NZL, NX, ROWS, 128), BF16),
            jax.ShapeDtypeStruct((2, NZH, 640, 128), BF16),
        ),
        in_specs=[pl.BlockSpec(memory_space=pltpu.SMEM)] + [vmem] * 6,
        out_specs=(hbm, hbm, hbm, hbm),
        scratch_shapes=[
            pltpu.VMEM((TOK, WIDTH), BF16),
            pltpu.VMEM((16, 3200), F32),
            pltpu.VMEM((GROUP, 7, 16, 128), BF16),
            pltpu.VMEM((DP, PAGE, 640), BF16),
            pltpu.VMEM((7, 128, 128), BF16),
            pltpu.VMEM((7, ROWS, 128), BF16),
            pltpu.VMEM((DP, PAGE, 640), BF16),
            pltpu.VMEM((KV_HEADS, 640, 128), BF16),
            pltpu.VMEM((2, 320, 128), BF16),
            pltpu.SemaphoreType.DMA((NSEM,)),
            pltpu.SemaphoreType.DMA((NSEM,)),
            pltpu.SemaphoreType.DMA((8,)),
        ],
        compiler_params=pltpu.CompilerParams(
            collective_id=0, has_side_effects=True, vmem_limit_bytes=40 * 1024 * 1024
        ),
        name="gather_all",
    )(slots, raw, gain, w_query, w_keyval, w_out, cache)


def attend_kernel(meta, x_ref, w_ref, kv_ref, cos_ref, sin_ref, out_ref, roped, kmat, vmat, qmat):
    c, length = meta[0], meta[1]
    x = x_ref[...].reshape(GROUP * TOK, WIDTH)
    lane = lax.broadcasted_iota(jnp.int32, (GROUP * TOK, 256), 1)
    early = lane % HEAD_DIM < HEAD_DIM // 2
    narrow = cos_ref[...]
    cosine = jnp.concatenate([narrow, pltpu.roll(narrow, 120, 1)], axis=1)
    narrow = sin_ref[...]
    sine = jnp.concatenate([narrow, pltpu.roll(narrow, 120, 1)], axis=1)
    sine = jnp.where(early, -sine, sine)
    for half in range(2):
        w = jnp.concatenate([w_ref[half, 0], w_ref[half, 1]], axis=1)
        raw = exact_dot(x, w)
        turned = jnp.where(early, pltpu.roll(raw, 216, 1), pltpu.roll(raw, 40, 1))
        new = raw * cosine + turned * sine
        if half == 1:
            new = jnp.where(lane < 160, new, raw)
        roped[half] = new.astype(BF16).reshape(NZH, 2, TOK, 256)
    row = lax.broadcasted_iota(jnp.int32, (512, 128), 0)
    lane = lax.broadcasted_iota(jnp.int32, (512, 128), 1)
    for cs in range(2):
        for zs in range(NZH):
            base = (cs * NZH + zs) * 512
            a = kv_ref[cs, zs, pl.ds(0, 512), :]
            position = (row // 16) * 128 + zs * 32 + cs * 16 + row % 16
            bias = jnp.where((lane == 80) & (position >= length), NEGATIVE, 0.0)
            kmat[pl.ds(base, 512), :] = jnp.where(lane < 80, a.astype(F32), bias).astype(BF16)
            vmat[pl.ds(base, 512), pl.ds(0, 128)] = a
            tail = kv_ref[cs, zs, pl.ds(512, 128), :]
            ones = jnp.where(lane[:128] == 32, 1.0, 0.0)
            for g in range(4):
                pick = one_hot(128, 128, lambda r, l: (l < 32) & (r == 32 * g + l))
                vmat[pl.ds(base + 128 * g, 128), pl.ds(128, 128)] = (
                    exact_dot(tail, pick) + ones
                ).astype(BF16)
    first = roped[0].reshape(512, 256)
    second = roped[1].reshape(512, 256)
    to_key = one_hot(256, 128, lambda r, l: (l < 80) & (r == 160 + l))
    kmat[pl.ds(4096, 512), :] = exact_dot(first, to_key).astype(BF16)
    to_value = one_hot(256, 256, lambda r, l: (l >= 80) & (l < 160) & (r == 80 + l))
    lane = lax.broadcasted_iota(jnp.int32, (512, 256), 1)
    ones = jnp.where(lane == 160, 1.0, 0.0)
    vmat[pl.ds(4096, 512), :] = (exact_dot(second, to_value) + ones).astype(BF16)

    lane = lax.broadcasted_iota(jnp.int32, (256, 128), 1)
    ones = jnp.where(lane == 80, 1.0, 0.0)
    own = [roped[half, :, c].reshape(256, 256) for half in range(2)]
    for h in range(4):
        off = HEAD_DIM * (h % 2)
        to_head = one_hot(256, 128, lambda r, l: (l < 80) & (r == off + l))
        qmat[h] = (exact_dot(own[h // 2], to_head) + ones).astype(BF16)

    row = lax.broadcasted_iota(jnp.int32, (256, 512), 0)
    col = lax.broadcasted_iota(jnp.int32, (256, 512), 1)
    token = (row // 64) * 128 + c * 64 + row % 64
    causal = jnp.where(col <= token, 0.0, NEGATIVE)
    scale = LOG2E * HEAD_DIM ** (-0.5)
    nt = (((1,), (1,)), ((), ()))

    out = exact_dot(
        own[0], one_hot(256, 512, lambda r, l: (l >= 320) & (l < 400) & (r == l - 160))
    ) + exact_dot(
        own[1], one_hot(256, 512, lambda r, l: (l >= 400) & (l < 480) & (r == l - 240))
    )
    for h in range(4):
        q = qmat[h]
        s = lax.dot_general(q, kmat[pl.ds(4096, 512), :], nt, preferred_element_type=F32) + causal
        top = jnp.max(s, axis=1, keepdims=True)
        p = jnp.exp2((s - top) * scale).astype(BF16)
        acc = exact_dot(p, vmat[pl.ds(4096, 512), :])
        for j in range(4):
            s = lax.dot_general(
                q, kmat[pl.ds(1024 * j, 1024), :], nt, preferred_element_type=F32
            )
            new_top = jnp.maximum(top, jnp.max(s, axis=1, keepdims=True))
            p = jnp.exp2((s - new_top) * scale).astype(BF16)
            acc = acc * jnp.exp2((top - new_top) * scale) + exact_dot(
                p, vmat[pl.ds(1024 * j, 1024), :]
            )
            top = new_top
        att = (acc / acc[:, 160:161]).astype(BF16)
        out = out + exact_dot(
            att,
            one_hot(256, 512, lambda r, l: (r >= 80) & (r < 160) & (l == 80 * h + r - 80)),
        )
    out_ref[...] = out.astype(BF16).reshape(NZH, TOK, 512)


def attend(meta, x, w, kv, cosine, sine):
    vmem = pl.BlockSpec(memory_space=pltpu.VMEM)
    return pl.pallas_call(
        attend_kernel,
        out_shape=jax.ShapeDtypeStruct((NZH, TOK, 512), BF16),
        in_specs=[pl.BlockSpec(memory_space=pltpu.SMEM), vmem, vmem, vmem, vmem, vmem],
        out_specs=vmem,
        scratch_shapes=[
            pltpu.VMEM((2, NZH, 2, TOK, 256), BF16),
            pltpu.VMEM((4608, 128), BF16),
            pltpu.VMEM((4608, 256), BF16),
            pltpu.VMEM((4, 256, 128), BF16),
        ],
        compiler_params=pltpu.CompilerParams(vmem_limit_bytes=30 * 1024 * 1024),
        name="attend",
    )(meta, x, w, kv, cosine, sine)


def project_kernel(msg, w, upd_ref, keyval_ref, rbuf, send, recv, local):
    dp = lax.axis_index("dp")
    f = lax.axis_index("fsdp")
    zh, c = f // 2, f % 2
    load = pltpu.make_async_copy(msg.at[zh], rbuf.at[zh], local.at[0])
    load.start()
    barrier = pltpu.get_barrier_semaphore()
    for d in range(1, NZH):
        g = (zh + d) % NZH
        pl.semaphore_signal(barrier, inc=1, device_id=(dp, g * 2 + c), device_id_type=MESH)
    pl.semaphore_wait(barrier, NZH - 1)
    copies = []
    for d in range(1, NZH):
        g = (zh + d) % NZH
        cp = pltpu.make_async_remote_copy(
            src_ref=msg.at[g],
            dst_ref=rbuf.at[zh],
            send_sem=send.at[d],
            recv_sem=recv.at[d],
            device_id=(dp, g * 2 + c),
            device_id_type=MESH,
        )
        cp.start()
        copies.append(cp)
    keyval = jnp.zeros((TOK, 640), F32)
    load.wait()
    for cp in copies:
        cp.wait_recv()
    lane = lax.broadcasted_iota(jnp.int32, (TOK, 128), 1)
    attended = []
    for pair in range(2):
        a = rbuf[2 * pair].astype(F32)
        b = pltpu.roll(rbuf[2 * pair + 1].astype(F32)[:, :384], 64, 1)
        attended += [
            a[:, 0:256],
            jnp.concatenate(
                [jnp.where(lane < 64, a[:, 256:384], b[:, 0:128]), b[:, 128:256]], axis=1
            ),
            b[:, 256:384],
        ]
    for k in range(KV_HEADS):

        def place(r, l, k=k):
            key = (r >= 64) & (r < 144) & (l == 80 * k + r - 64)
            value = (r >= 144) & (r < 224) & (l == 320 + 80 * k + r - 144)
            return key | value

        keyval = keyval + exact_dot(rbuf[k][:, 256:512], one_hot(256, 640, place))
    keyval_ref[...] = keyval.astype(BF16)
    tiles = [t.astype(BF16) for t in attended]
    nt = (((1,), (1,)), ((), ()))
    spans = ((0, 2), (2, 2), (4, 1), (5, 2), (7, 2), (9, 1))
    for n in range(4):
        rows = pl.ds(640 * n, 640)
        total = jnp.zeros((TOK, 640), F32)
        for t, (lo, count) in zip(tiles, spans):
            parts = [w[(lo + i) // 5, (lo + i) % 5, rows, :] for i in range(count)]
            rhs = parts[0] if count == 1 else jnp.concatenate(parts, axis=1)
            total = total + lax.dot_general(t, rhs, nt, preferred_element_type=F32)
        upd_ref[:, 640 * n : 640 * n + 640] = total.astype(BF16)
    for cp in copies:
        cp.wait_send()


def project(msg, w):
    vmem = pl.BlockSpec(memory_space=pltpu.VMEM)
    return pl.pallas_call(
        project_kernel,
        out_shape=(
            jax.ShapeDtypeStruct((TOK, WIDTH), BF16),
            jax.ShapeDtypeStruct((TOK, 640), BF16),
        ),
        in_specs=[pl.BlockSpec(memory_space=pl.ANY), vmem],
        out_specs=(vmem, vmem),
        scratch_shapes=[
            pltpu.VMEM((NZH, TOK, 512), BF16),
            pltpu.SemaphoreType.DMA((4,)),
            pltpu.SemaphoreType.DMA((4,)),
            pltpu.SemaphoreType.DMA((1,)),
        ],
        compiler_params=pltpu.CompilerParams(
            collective_id=1, has_side_effects=True, vmem_limit_bytes=20 * 1024 * 1024
        ),
        name="project",
    )(msg, w)


def on_device(
    stretch_tokens, norm_gain, w_query, w_keyval, w_out, cache_store, cache_lengths, source_slot
):
    dp = lax.axis_index("dp")
    f = lax.axis_index("fsdp")
    length = cache_lengths[source_slot[dp]]
    toks_all, w_qkv, w_o, kv = gather_all(
        source_slot,
        stretch_tokens[0],
        norm_gain[None],
        w_query,
        w_keyval,
        w_out,
        cache_store,
    )
    half = HEAD_DIM // 2
    feature = (jnp.arange(128, dtype=jnp.int32) % half).astype(F32)
    frequency = ROPE_BASE ** (-(feature * 2.0) / HEAD_DIM)
    positions = length + jnp.arange(GROUP * TOK, dtype=jnp.int32)
    angles = positions.astype(F32)[:, None] * frequency
    cosine, sine = jnp.cos(angles), jnp.sin(angles)

    meta = jnp.stack([f % 2, length]).astype(jnp.int32)
    msg = attend(meta, toks_all, w_qkv.reshape(2, 2, WIDTH, 128), kv, cosine, sine)
    update, new_keyval = project(msg, w_o.reshape(2, 5, WIDTH, 128))
    return (update[None], new_keyval[None])


def solution(mesh):
    in_specs = (
        P("dp", "fsdp", None),
        P(),
        P(("dp", "fsdp"), None),
        P(("dp", "fsdp"), None),
        P(("dp", "fsdp"), None),
        P(None, ("dp", "fsdp"), None),
        P(),
        P(),
    )
    out_specs = (P("dp", "fsdp", None), P("dp", "fsdp", None))
    return jax.shard_map(
        on_device, mesh=mesh, in_specs=in_specs, out_specs=out_specs, check_vma=False
    )
```

```python
import functools

import jax
import jax.numpy as jnp
import numpy as np
from jax import lax
from jax.experimental import pallas as pl
from jax.experimental.pallas import tpu as pltpu
from jax.sharding import PartitionSpec as P

MESH = pl.DeviceIdType.MESH
BF16 = jnp.bfloat16
F32 = jnp.float32

HEAD_DIM = 80
HEADS = 16
KV_HEADS = 4
ROPE_BASE = 1000000.0
EPSILON = 1e-05
NEGATIVE = -1e30
LOG2E = 1.4426950408889634

NX, NY, NZL, NZH = 4, 4, 2, 4
DP, GROUP = 32, 8
TOK = 64
WIDTH = 2560
PAGE = 16
ROWS = 80
S1ROWS = 10

UNITS = ((0, 0, 1, 0), (0, 1, 1, 1), (1, 0, 3, 0), (1, 3, 2, 1))

S1 = 0
S2 = 8
TK = 10
CX = 20
RING = 36
PER_UNIT = 13
C1 = RING + PER_UNIT * len(UNITS)
NSEM = C1 + DP


def one_hot(rows, columns, test):
    r = lax.broadcasted_iota(jnp.int32, (rows, columns), 0)
    l = lax.broadcasted_iota(jnp.int32, (rows, columns), 1)
    return jnp.where(test(r, l), 1.0, 0.0).astype(BF16)


def exact_dot(a, b):
    return jnp.dot(a, b, preferred_element_type=F32)


def gather_kernel(
    slots, lengths, raw_hbm, gain, wq_hbm, wkv_hbm, wo_hbm, cache_hbm,
    toks_all, w_qkv, w_out, kv, cos_ref, sin_ref,
    raw, wq_ref, wkv_ref, wo_ref, cache_ref, loads, tok, stage, wp, cache, s1buf, blk, cbuf, pack, relay, send, recv, local
):
    dp = lax.axis_index("dp")
    f = lax.axis_index("fsdp")
    y, rest = dp // 8, dp % 8
    zl, x = rest // 4, rest % 4
    zh, c = f // 2, f % 2

    def dp_of(yy, zz, xx):
        return (yy * 2 + zz) * 4 + xx

    sources = ((raw_hbm, raw), (wq_hbm, wq_ref), (wkv_hbm, wkv_ref), (wo_hbm, wo_ref))
    sources += ((cache_hbm, cache_ref),)
    loading = [
        pltpu.make_async_copy(src, dst, loads.at[i]) for i, (src, dst) in enumerate(sources)
    ]
    for cp in loading:
        cp.start()
    s1buf[...] = jnp.zeros_like(s1buf)
    barrier = pltpu.get_barrier_semaphore()

    def greet_group(d, carry):
        pl.semaphore_signal(
            barrier, inc=1, device_id=(dp, (f + d) % GROUP), device_id_type=MESH
        )
        return carry

    def greet_data(d, carry):
        pl.semaphore_signal(barrier, inc=1, device_id=((dp + d) % DP, f), device_id_type=MESH)
        return carry

    lax.fori_loop(1, GROUP, greet_group, 0)
    lax.fori_loop(1, DP, greet_data, 0)

    stage[...] = jnp.zeros_like(stage)
    for cp in loading:
        cp.wait()
    tokens = raw[...].astype(F32)
    squares = jnp.mean(tokens * tokens, axis=-1, keepdims=True)
    tok[...] = (tokens * lax.rsqrt(squares + EPSILON) * gain[...].astype(F32)).astype(BF16)
    stage[pl.ds(0, 10), pl.ds(0, 1280)] = wq_ref[...].astype(F32)
    stage[pl.ds(0, 10), pl.ds(1280, 640)] = wkv_ref[...].astype(F32)
    stage[pl.ds(0, 10), pl.ds(1920, 1280)] = wo_ref[...].astype(F32)
    lane = lax.broadcasted_iota(jnp.int32, (16, 256), 1)
    for g in range(GROUP):
        k, half = g // 2, g % 2
        start = 160 * g
        base = start // 128 * 128
        q = stage[:, base : base + 256]
        if start > base:
            q = pltpu.roll(q, 256 - (start - base), 1)
        start = 320 * half + HEAD_DIM * k
        base = min(start // 128 * 128, 384)
        rest_ = stage[:, 1280 + base : 1536 + base]
        shift = (160 - (start - base)) % 256
        if shift:
            rest_ = pltpu.roll(rest_, shift, 1)
        both = jnp.where(lane < 160, q, jnp.where(lane < 240, rest_, 0.0)).astype(BF16)
        wp[g, 0] = both[:, :128]
        wp[g, 1] = both[:, 128:]
        for t in range(5):
            at = 1920 + 640 * half + 128 * t
            wp[g, 2 + t] = stage[:, at : at + 128].astype(BF16)
    for slot in range(DP):
        cache[slot] = cache_ref[slots[slot]]
    pl.semaphore_wait(barrier, GROUP - 1 + DP - 1)

    started = []

    def rcopy(src, dst, sem, dev):
        cp = pltpu.make_async_remote_copy(
            src_ref=src,
            dst_ref=dst,
            send_sem=send.at[sem],
            recv_sem=recv.at[sem],
            device_id=dev,
            device_id_type=MESH,
        )
        cp.start()
        started.append(cp)
        return cp

    nlocal = [0]

    def lcopy(src, dst):
        cp = pltpu.make_async_copy(src, dst, local.at[nlocal[0]])
        nlocal[0] += 1
        cp.start()
        return cp

    twin = (dp, zh * 2 + 1 - c)

    s1 = []
    for d in range(1, GROUP):
        g = (f + d) % GROUP
        s1.append(
            rcopy(
                wp.at[g, :, pl.ds(0, S1ROWS), :],
                s1buf.at[:, pl.ds(pl.multiple_of(f * 16, 16), S1ROWS), :],
                S1 + d,
                (dp, g),
            )
        )
    zp, zm = (zh + 1) % NZH, (zh + NZH - 1) % NZH
    zo = (zh + 2) % NZH
    t0 = rcopy(tok, toks_all.at[f], TK + 0, (dp, zp * 2 + c))
    t1 = rcopy(tok, toks_all.at[f], TK + 1, (dp, zm * 2 + c))
    t4 = rcopy(tok, toks_all.at[f], TK + 4, twin)
    tl = lcopy(tok, toks_all.at[f])

    def page_copy(d):
        there = (dp + d) % DP
        return pltpu.make_async_remote_copy(
            src_ref=cache.at[there],
            dst_ref=cbuf.at[dp],
            send_sem=send.at[C1 + d],
            recv_sem=recv.at[C1 + d],
            device_id=(there, f),
            device_id_type=MESH,
        )

    def page_start(d, carry):
        page_copy(d).start()
        return carry

    lax.fori_loop(1, DP, page_start, 0)
    cbuf[dp] = cache[dp]

    length = lengths[slots[dp]]
    feature = lax.broadcasted_iota(jnp.int32, (TOK, 128), 1) % (HEAD_DIM // 2)
    frequency = jnp.zeros((TOK, 128), F32)
    for i in range(HEAD_DIM // 2):
        value = np.float32(ROPE_BASE) ** np.float32(-2.0 * i / HEAD_DIM)
        frequency = jnp.where(feature == i, float(value), frequency)

    def table(i, carry):
        position = length + i * TOK + lax.broadcasted_iota(jnp.int32, (TOK, 128), 0)
        angles = position.astype(F32) * frequency
        rows = pl.ds(pl.multiple_of(i * TOK, TOK), TOK)
        cos_ref[rows, :] = jnp.cos(angles)
        sin_ref[rows, :] = jnp.sin(angles)
        return carry

    s1buf[:, pl.ds(pl.multiple_of(f * 16, 16), 16), :] = wp[f]
    for cp in s1:
        cp.wait_recv()
    squeeze = one_hot(ROWS, 128, lambda r, l: l == 16 * (r // 10) + r % 10)
    for t in range(7):
        blk[t] = exact_dot(squeeze, s1buf[t]).astype(BF16)

    there = dp_of(y, 1 - zl, x)
    mine_q = w_qkv.at[c, :, y, zl, x]
    mine_o = w_out.at[c, :, y, zl, x]
    q2 = rcopy(blk.at[pl.ds(0, 2)], mine_q, S2 + 0, (there, f))
    lq = lcopy(blk.at[pl.ds(0, 2)], mine_q)
    o2 = rcopy(blk.at[pl.ds(2, 5)], mine_o, S2 + 1, (there, f))
    lo = lcopy(blk.at[pl.ds(2, 5)], mine_o)

    xp, xm, xo = (x + 1) % NX, (x + NX - 1) % NX, (x + 2) % NX
    yp, ym, yo = (y + 1) % NY, (y + NY - 1) % NY, (y + 2) % NY
    devices = {
        0: ((dp_of(y, zl, xp), f), (dp_of(y, zl, xm), f)),
        1: ((dp_of(yp, zl, x), f), (dp_of(ym, zl, x), f)),
    }
    along = {0: (x, xm, xp, xo), 1: (y, ym, yp, yo)}

    def near(unit, at, half=None):
        which, lo_, n, axis = unit
        arr = (w_qkv, w_out)[which]
        z = slice(None) if half is None else half
        if axis == 0:
            return arr.at[c, pl.ds(lo_, n), y, z, at]
        return arr.at[c, pl.ds(lo_, n), at, z, x]

    def far(unit, at, half=None):
        which, lo_, n, axis = unit
        arr = (w_qkv, w_out)[which]
        z = slice(None) if half is None else half
        if axis == 0:
            return arr.at[c, pl.ds(lo_, n), at, z]
        return arr.at[c, pl.ds(lo_, n), :, z, at]

    class Ring:
        def __init__(self, u, second):
            self.unit = UNITS[u]
            self.base = RING + PER_UNIT * u + (4 if second else 0)
            self.axis = self.unit[3] if not second else 1 - self.unit[3]
            self.part = far if second else near
            self.at, self.minus, self.plus, self.other = along[self.axis]

        def start(self):
            up, down = devices[self.axis]
            own = self.part(self.unit, self.at)
            self.a = rcopy(own, own, self.base + 0, up)
            self.b = rcopy(own, own, self.base + 1, down)

        def relay(self):
            up, down = devices[self.axis]
            self.a.wait_recv()
            piece = self.part(self.unit, self.minus, 0)
            self.c = rcopy(piece, piece, self.base + 2, up)
            self.b.wait_recv()
            piece = self.part(self.unit, self.plus, 1)
            self.d = rcopy(piece, piece, self.base + 3, down)

        def finish(self):
            self.c.wait_recv()
            self.d.wait_recv()

    firsts = [Ring(u, False) for u in range(4)]
    seconds = [Ring(u, True) for u in range(4)]
    hands = []

    def hand(u, k, ref):
        hands.append(rcopy(ref, ref, RING + PER_UNIT * u + 8 + k, twin))

    def hand_own(u):
        hand(u, 0, far(UNITS[u], seconds[u].at))

    def hand_next(u):
        s = seconds[u]
        hand(u, 1, far(UNITS[u], s.minus))
        hand(u, 2, far(UNITS[u], s.plus))

    def hand_last(u):
        s = seconds[u]
        hand(u, 3, far(UNITS[u], s.other, 0))
        hand(u, 4, far(UNITS[u], s.other, 1))

    q2.wait_recv()
    lq.wait()
    firsts[0].start()
    firsts[1].start()
    o2.wait_recv()
    lo.wait()
    firsts[2].start()
    firsts[3].start()
    firsts[0].relay()
    firsts[1].relay()
    for u in (0, 1):
        firsts[u].finish()
        seconds[u].start()
        hand_own(u)
    firsts[2].relay()
    firsts[3].relay()
    for u in (2, 3):
        firsts[u].finish()
        seconds[u].start()
        hand_own(u)

    t0.wait_recv()
    ref = toks_all.at[zm * 2 + c]
    t2 = rcopy(
        toks_all.at[zm * 2 + c, pl.ds(0, 32)],
        toks_all.at[zm * 2 + c, pl.ds(0, 32)],
        TK + 2,
        (dp, zp * 2 + c),
    )
    t5 = rcopy(ref, ref, TK + 5, twin)
    t1.wait_recv()
    ref = toks_all.at[zp * 2 + c]
    t3 = rcopy(
        toks_all.at[zp * 2 + c, pl.ds(32, 32)],
        toks_all.at[zp * 2 + c, pl.ds(32, 32)],
        TK + 3,
        (dp, zm * 2 + c),
    )
    t6 = rcopy(ref, ref, TK + 6, twin)

    lax.fori_loop(0, GROUP, table, 0)

    def page_wait(d, carry):
        page_copy(d).wait_recv()
        return carry

    lax.fori_loop(1, DP, page_wait, 0)
    pages = cbuf[...].reshape(DP * PAGE, 2 * KV_HEADS * HEAD_DIM)
    for k in range(KV_HEADS):

        def pick(r, l, k=k):
            value = KV_HEADS * HEAD_DIM + HEAD_DIM * k
            key = (l < 80) & (r == HEAD_DIM * k + l)
            front = (l >= 80) & (l < 128) & (r == value + l - 80)
            back = (l >= 128) & (r == value + 48 + l % 32)
            return key | front | back

        both = exact_dot(pages, one_hot(640, 256, pick))
        pack[k, pl.ds(0, 512), :] = both[:, :128].astype(BF16)
        lane = lax.broadcasted_iota(jnp.int32, (128, 128), 1) // 32
        tail = jnp.zeros((128, 128), F32)
        for g in range(4):
            tail = jnp.where(lane == g, both[128 * g : 128 * g + 128, 128:], tail)
        pack[k, pl.ds(512, 128), :] = tail.astype(BF16)
    up, down = (dp, zp * 2 + c), (dp, zm * 2 + c)
    h0 = rcopy(pack.at[zp], kv.at[c, zh], CX + 0, up)
    h1 = rcopy(pack.at[zm], kv.at[c, zh], CX + 1, down)
    h2 = rcopy(pack.at[zo, pl.ds(0, 320)], relay.at[0], CX + 2, up)
    h3 = rcopy(pack.at[zo, pl.ds(320, 320)], relay.at[1], CX + 3, down)
    hl = lcopy(pack.at[zh], kv.at[c, zh])
    hands.append(rcopy(pack.at[zh], kv.at[c, zh], CX + 6, twin))

    for u in (0, 1):
        seconds[u].relay()
        hand_next(u)
    h2.wait_recv()
    h4 = rcopy(relay.at[0], kv.at[c, zm, pl.ds(0, 320)], CX + 4, up)
    h3.wait_recv()
    h5 = rcopy(relay.at[1], kv.at[c, zp, pl.ds(320, 320)], CX + 5, down)
    for u in (2, 3):
        seconds[u].relay()
        hand_next(u)
    t2.wait_recv()
    ref = toks_all.at[zo * 2 + c, pl.ds(0, 32)]
    t7 = rcopy(ref, ref, TK + 7, twin)
    t3.wait_recv()
    ref = toks_all.at[zo * 2 + c, pl.ds(32, 32)]
    t8 = rcopy(ref, ref, TK + 8, twin)
    for u in (0, 1):
        seconds[u].finish()
        hand_last(u)
    h0.wait_recv()
    ref = kv.at[c, zm]
    hands.append(rcopy(ref, ref, CX + 7, twin))
    h1.wait_recv()
    ref = kv.at[c, zp]
    hands.append(rcopy(ref, ref, CX + 8, twin))
    h4.wait_recv()
    ref = kv.at[c, zo, pl.ds(0, 320)]
    hands.append(rcopy(ref, ref, CX + 9, twin))
    h5.wait_recv()
    ref = kv.at[c, zo, pl.ds(320, 320)]
    hands.append(rcopy(ref, ref, CX + 10, twin))
    for u in (2, 3):
        seconds[u].finish()
        hand_last(u)

    for cp in (t4, t5, t6, t7, t8, *hands):
        cp.wait_recv()
    for cp in started:
        cp.wait_send()

    def page_sent(d, carry):
        page_copy(d).wait_send()
        return carry

    lax.fori_loop(1, DP, page_sent, 0)
    tl.wait()
    hl.wait()


def gather_all(slots, lengths, raw, gain, w_query, w_keyval, w_out, cache):
    vmem = pl.BlockSpec(memory_space=pltpu.VMEM)
    hbm = pl.BlockSpec(memory_space=pl.ANY)
    far = pl.BlockSpec(memory_space=pltpu.HBM)
    return pl.pallas_call(
        gather_kernel,
        out_shape=(
            jax.ShapeDtypeStruct((GROUP, TOK, WIDTH), BF16),
            jax.ShapeDtypeStruct((2, 2, NY, NZL, NX, ROWS, 128), BF16),
            jax.ShapeDtypeStruct((2, 5, NY, NZL, NX, ROWS, 128), BF16),
            jax.ShapeDtypeStruct((2, NZH, 640, 128), BF16),
            jax.ShapeDtypeStruct((GROUP * TOK, 128), F32),
            jax.ShapeDtypeStruct((GROUP * TOK, 128), F32),
        ),
        in_specs=[pl.BlockSpec(memory_space=pltpu.SMEM)] * 2 + [far, vmem] + [far] * 4,
        out_specs=(hbm, hbm, hbm, hbm, vmem, vmem),
        scratch_shapes=[
            pltpu.VMEM((TOK, WIDTH), BF16),
            pltpu.VMEM((10, 1280), BF16),
            pltpu.VMEM((10, 640), BF16),
            pltpu.VMEM((10, 1280), BF16),
            pltpu.VMEM((DP, PAGE, 640), BF16),
            pltpu.SemaphoreType.DMA((5,)),
            pltpu.VMEM((TOK, WIDTH), BF16),
            pltpu.VMEM((16, 3200), F32),
            pltpu.VMEM((GROUP, 7, 16, 128), BF16),
            pltpu.VMEM((DP, PAGE, 640), BF16),
            pltpu.VMEM((7, 128, 128), BF16),
            pltpu.VMEM((7, ROWS, 128), BF16),
            pltpu.VMEM((DP, PAGE, 640), BF16),
            pltpu.VMEM((KV_HEADS, 640, 128), BF16),
            pltpu.VMEM((2, 320, 128), BF16),
            pltpu.SemaphoreType.DMA((NSEM,)),
            pltpu.SemaphoreType.DMA((NSEM,)),
            pltpu.SemaphoreType.DMA((8,)),
        ],
        compiler_params=pltpu.CompilerParams(
            collective_id=0, has_side_effects=True, vmem_limit_bytes=40 * 1024 * 1024
        ),
        name="gather_all",
    )(slots, lengths, raw, gain, w_query, w_keyval, w_out, cache)


def attend_kernel(
    slots, lengths, x_ref, w_ref, kv_ref, cos_ref, sin_ref, out_ref, roped, kmat, vmat, qmat
):
    c, length = lax.axis_index("fsdp") % 2, lengths[slots[lax.axis_index("dp")]]
    x = x_ref[...].reshape(GROUP * TOK, WIDTH)
    lane = lax.broadcasted_iota(jnp.int32, (GROUP * TOK, 256), 1)
    early = lane % HEAD_DIM < HEAD_DIM // 2
    narrow = cos_ref[...]
    cosine = jnp.concatenate([narrow, pltpu.roll(narrow, 120, 1)], axis=1)
    narrow = sin_ref[...]
    sine = jnp.concatenate([narrow, pltpu.roll(narrow, 120, 1)], axis=1)
    sine = jnp.where(early, -sine, sine)
    for half in range(2):
        w = jnp.concatenate([w_ref[half, 0], w_ref[half, 1]], axis=1)
        raw = exact_dot(x, w)
        turned = jnp.where(early, pltpu.roll(raw, 216, 1), pltpu.roll(raw, 40, 1))
        new = raw * cosine + turned * sine
        if half == 1:
            new = jnp.where(lane < 160, new, raw)
        roped[half] = new.astype(BF16).reshape(NZH, 2, TOK, 256)
    row = lax.broadcasted_iota(jnp.int32, (512, 128), 0)
    lane = lax.broadcasted_iota(jnp.int32, (512, 128), 1)
    for cs in range(2):
        for zs in range(NZH):
            base = (cs * NZH + zs) * 512
            a = kv_ref[cs, zs, pl.ds(0, 512), :]
            position = (row // 16) * 128 + zs * 32 + cs * 16 + row % 16
            bias = jnp.where((lane == 80) & (position >= length), NEGATIVE, 0.0)
            kmat[pl.ds(base, 512), :] = jnp.where(lane < 80, a.astype(F32), bias).astype(BF16)
            vmat[pl.ds(base, 512), pl.ds(0, 128)] = a
            tail = kv_ref[cs, zs, pl.ds(512, 128), :]
            ones = jnp.where(lane[:128] == 32, 1.0, 0.0)
            for g in range(4):
                pick = one_hot(128, 128, lambda r, l: (l < 32) & (r == 32 * g + l))
                vmat[pl.ds(base + 128 * g, 128), pl.ds(128, 128)] = (
                    exact_dot(tail, pick) + ones
                ).astype(BF16)
    first = roped[0].reshape(512, 256)
    second = roped[1].reshape(512, 256)
    to_key = one_hot(256, 128, lambda r, l: (l < 80) & (r == 160 + l))
    kmat[pl.ds(4096, 512), :] = exact_dot(first, to_key).astype(BF16)
    to_value = one_hot(256, 256, lambda r, l: (l >= 80) & (l < 160) & (r == 80 + l))
    lane = lax.broadcasted_iota(jnp.int32, (512, 256), 1)
    ones = jnp.where(lane == 160, 1.0, 0.0)
    vmat[pl.ds(4096, 512), :] = (exact_dot(second, to_value) + ones).astype(BF16)

    lane = lax.broadcasted_iota(jnp.int32, (256, 128), 1)
    ones = jnp.where(lane == 80, 1.0, 0.0)
    own = [roped[half, :, c].reshape(256, 256) for half in range(2)]
    for h in range(4):
        off = HEAD_DIM * (h % 2)
        to_head = one_hot(256, 128, lambda r, l: (l < 80) & (r == off + l))
        qmat[h] = (exact_dot(own[h // 2], to_head) + ones).astype(BF16)

    row = lax.broadcasted_iota(jnp.int32, (256, 512), 0)
    col = lax.broadcasted_iota(jnp.int32, (256, 512), 1)
    token = (row // 64) * 128 + c * 64 + row % 64
    causal = jnp.where(col <= token, 0.0, NEGATIVE)
    scale = LOG2E * HEAD_DIM ** (-0.5)
    nt = (((1,), (1,)), ((), ()))

    out = exact_dot(
        own[0], one_hot(256, 512, lambda r, l: (l >= 320) & (l < 400) & (r == l - 160))
    ) + exact_dot(
        own[1], one_hot(256, 512, lambda r, l: (l >= 400) & (l < 480) & (r == l - 240))
    )
    for h in range(4):
        q = qmat[h]
        s = lax.dot_general(q, kmat[pl.ds(4096, 512), :], nt, preferred_element_type=F32) + causal
        top = jnp.max(s, axis=1, keepdims=True)
        p = jnp.exp2((s - top) * scale).astype(BF16)
        acc = exact_dot(p, vmat[pl.ds(4096, 512), :])
        for j in range(4):
            s = lax.dot_general(
                q, kmat[pl.ds(1024 * j, 1024), :], nt, preferred_element_type=F32
            )
            new_top = jnp.maximum(top, jnp.max(s, axis=1, keepdims=True))
            p = jnp.exp2((s - new_top) * scale).astype(BF16)
            acc = acc * jnp.exp2((top - new_top) * scale) + exact_dot(
                p, vmat[pl.ds(1024 * j, 1024), :]
            )
            top = new_top
        att = (acc / acc[:, 160:161]).astype(BF16)
        out = out + exact_dot(
            att,
            one_hot(256, 512, lambda r, l: (r >= 80) & (r < 160) & (l == 80 * h + r - 80)),
        )
    out_ref[...] = out.astype(BF16).reshape(NZH, TOK, 512)


def attend(slots, lengths, x, w, kv, cosine, sine):
    vmem = pl.BlockSpec(memory_space=pltpu.VMEM)
    return pl.pallas_call(
        attend_kernel,
        out_shape=jax.ShapeDtypeStruct((NZH, TOK, 512), BF16),
        in_specs=[pl.BlockSpec(memory_space=pltpu.SMEM)] * 2 + [vmem] * 5,
        out_specs=vmem,
        scratch_shapes=[
            pltpu.VMEM((2, NZH, 2, TOK, 256), BF16),
            pltpu.VMEM((4608, 128), BF16),
            pltpu.VMEM((4608, 256), BF16),
            pltpu.VMEM((4, 256, 128), BF16),
        ],
        compiler_params=pltpu.CompilerParams(vmem_limit_bytes=30 * 1024 * 1024),
        name="attend",
    )(slots, lengths, x, w, kv, cosine, sine)


def project_kernel(msg, w, upd_hbm, keyval_hbm, rbuf, upd_ref, keyval_ref, send, recv, local):
    dp = lax.axis_index("dp")
    f = lax.axis_index("fsdp")
    zh, c = f // 2, f % 2
    load = pltpu.make_async_copy(msg.at[zh], rbuf.at[zh], local.at[0])
    load.start()
    barrier = pltpu.get_barrier_semaphore()
    for d in range(1, NZH):
        g = (zh + d) % NZH
        pl.semaphore_signal(barrier, inc=1, device_id=(dp, g * 2 + c), device_id_type=MESH)
    pl.semaphore_wait(barrier, NZH - 1)
    copies = []
    for d in range(1, NZH):
        g = (zh + d) % NZH
        cp = pltpu.make_async_remote_copy(
            src_ref=msg.at[g],
            dst_ref=rbuf.at[zh],
            send_sem=send.at[d],
            recv_sem=recv.at[d],
            device_id=(dp, g * 2 + c),
            device_id_type=MESH,
        )
        cp.start()
        copies.append(cp)
    keyval = jnp.zeros((TOK, 640), F32)
    load.wait()
    for cp in copies:
        cp.wait_recv()
    lane = lax.broadcasted_iota(jnp.int32, (TOK, 128), 1)
    attended = []
    for pair in range(2):
        a = rbuf[2 * pair].astype(F32)
        b = pltpu.roll(rbuf[2 * pair + 1].astype(F32)[:, :384], 64, 1)
        attended += [
            a[:, 0:256],
            jnp.concatenate(
                [jnp.where(lane < 64, a[:, 256:384], b[:, 0:128]), b[:, 128:256]], axis=1
            ),
            b[:, 256:384],
        ]
    for k in range(KV_HEADS):

        def place(r, l, k=k):
            key = (r >= 64) & (r < 144) & (l == 80 * k + r - 64)
            value = (r >= 144) & (r < 224) & (l == 320 + 80 * k + r - 144)
            return key | value

        keyval = keyval + exact_dot(rbuf[k][:, 256:512], one_hot(256, 640, place))
    keyval_ref[...] = keyval.astype(BF16)
    stores = [pltpu.make_async_copy(keyval_ref, keyval_hbm, local.at[1])]
    stores[0].start()
    tiles = [t.astype(BF16) for t in attended]
    nt = (((1,), (1,)), ((), ()))
    spans = ((0, 2), (2, 2), (4, 1), (5, 2), (7, 2), (9, 1))
    for n in range(4):
        rows = pl.ds(640 * n, 640)
        total = jnp.zeros((TOK, 640), F32)
        for t, (lo, count) in zip(tiles, spans):
            parts = [w[(lo + i) // 5, (lo + i) % 5, rows, :] for i in range(count)]
            rhs = parts[0] if count == 1 else jnp.concatenate(parts, axis=1)
            total = total + lax.dot_general(t, rhs, nt, preferred_element_type=F32)
        upd_ref[:, 640 * n : 640 * n + 640] = total.astype(BF16)
        cols = pl.ds(640 * n, 640)
        cp = pltpu.make_async_copy(upd_ref.at[:, cols], upd_hbm.at[:, cols], local.at[2 + n])
        cp.start()
        stores.append(cp)
    for cp in copies:
        cp.wait_send()
    for cp in stores:
        cp.wait()


def project(msg, w):
    vmem = pl.BlockSpec(memory_space=pltpu.VMEM)
    far = pl.BlockSpec(memory_space=pltpu.HBM)
    return pl.pallas_call(
        project_kernel,
        out_shape=(
            jax.ShapeDtypeStruct((TOK, WIDTH), BF16),
            jax.ShapeDtypeStruct((TOK, 640), BF16),
        ),
        in_specs=[pl.BlockSpec(memory_space=pl.ANY), vmem],
        out_specs=(far, far),
        scratch_shapes=[
            pltpu.VMEM((NZH, TOK, 512), BF16),
            pltpu.VMEM((TOK, WIDTH), BF16),
            pltpu.VMEM((TOK, 640), BF16),
            pltpu.SemaphoreType.DMA((4,)),
            pltpu.SemaphoreType.DMA((4,)),
            pltpu.SemaphoreType.DMA((6,)),
        ],
        compiler_params=pltpu.CompilerParams(
            collective_id=1, has_side_effects=True, vmem_limit_bytes=20 * 1024 * 1024
        ),
        name="project",
    )(msg, w)


def on_device(
    stretch_tokens, norm_gain, w_query, w_keyval, w_out, cache_store, cache_lengths, source_slot
):
    toks_all, w_qkv, w_o, kv, cosine, sine = gather_all(
        source_slot,
        cache_lengths,
        stretch_tokens[0],
        norm_gain[None],
        w_query,
        w_keyval,
        w_out,
        cache_store,
    )
    qkv = w_qkv.reshape(2, 2, WIDTH, 128)
    msg = attend(source_slot, cache_lengths, toks_all, qkv, kv, cosine, sine)
    update, new_keyval = project(msg, w_o.reshape(2, 5, WIDTH, 128))
    return (update[None], new_keyval[None])


def solution(mesh):
    in_specs = (
        P("dp", "fsdp", None),
        P(),
        P(("dp", "fsdp"), None),
        P(("dp", "fsdp"), None),
        P(("dp", "fsdp"), None),
        P(None, ("dp", "fsdp"), None),
        P(),
        P(),
    )
    out_specs = (P("dp", "fsdp", None), P("dp", "fsdp", None))
    return jax.shard_map(
        on_device, mesh=mesh, in_specs=in_specs, out_specs=out_specs, check_vma=False
    )
```

```python
import functools

import jax
import jax.numpy as jnp
import numpy as np
from jax import lax
from jax.experimental import pallas as pl
from jax.experimental.pallas import tpu as pltpu
from jax.sharding import PartitionSpec as P

MESH = pl.DeviceIdType.MESH
BF16 = jnp.bfloat16
F32 = jnp.float32

HEAD_DIM = 80
HEADS = 16
KV_HEADS = 4
ROPE_BASE = 1000000.0
EPSILON = 1e-05
NEGATIVE = -1e30
LOG2E = 1.4426950408889634

NX, NY, NZL, NZH = 4, 4, 2, 4
DP, GROUP = 32, 8
TOK = 64
WIDTH = 2560
PAGE = 16
ROWS = 80
S1ROWS = 10

UNITS = ((0, 0, 1, 0), (0, 1, 1, 1), (1, 0, 3, 0), (1, 3, 2, 1))

S1 = 0
S2 = 8
TK = 10
CX = 20
RING = 36
PER_UNIT = 13
C1 = RING + PER_UNIT * len(UNITS)
NSEM = C1 + DP


def one_hot(rows, columns, test):
    r = lax.broadcasted_iota(jnp.int32, (rows, columns), 0)
    l = lax.broadcasted_iota(jnp.int32, (rows, columns), 1)
    return jnp.where(test(r, l), 1.0, 0.0).astype(BF16)


def exact_dot(a, b):
    return jnp.dot(a, b, preferred_element_type=F32)


def gather_kernel(
    slots, lengths, raw_hbm, gain, wq_hbm, wkv_hbm, wo_hbm, cache_hbm,
    toks_all, w_qkv, w_out, kv, cos_ref, sin_ref, length_ref,
    raw, wq_ref, wkv_ref, wo_ref, cache_ref, loads, tok, stage, wp, cache, s1buf, blk, cbuf, pack, relay, send, recv, local
):
    dp = lax.axis_index("dp")
    f = lax.axis_index("fsdp")
    y, rest = dp // 8, dp % 8
    zl, x = rest // 4, rest % 4
    zh, c = f // 2, f % 2

    def dp_of(yy, zz, xx):
        return (yy * 2 + zz) * 4 + xx

    sources = ((raw_hbm, raw), (wq_hbm, wq_ref), (wkv_hbm, wkv_ref), (wo_hbm, wo_ref))
    sources += ((cache_hbm, cache_ref),)
    loading = [
        pltpu.make_async_copy(src, dst, loads.at[i]) for i, (src, dst) in enumerate(sources)
    ]
    for cp in loading:
        cp.start()
    s1buf[...] = jnp.zeros_like(s1buf)
    barrier = pltpu.get_barrier_semaphore()

    def greet_group(d, carry):
        pl.semaphore_signal(
            barrier, inc=1, device_id=(dp, (f + d) % GROUP), device_id_type=MESH
        )
        return carry

    def greet_data(d, carry):
        pl.semaphore_signal(barrier, inc=1, device_id=((dp + d) % DP, f), device_id_type=MESH)
        return carry

    lax.fori_loop(1, GROUP, greet_group, 0)
    lax.fori_loop(1, DP, greet_data, 0)

    stage[...] = jnp.zeros_like(stage)
    for cp in loading:
        cp.wait()
    tokens = raw[...].astype(F32)
    squares = jnp.mean(tokens * tokens, axis=-1, keepdims=True)
    tok[...] = (tokens * lax.rsqrt(squares + EPSILON) * gain[...].astype(F32)).astype(BF16)
    stage[pl.ds(0, 10), pl.ds(0, 1280)] = wq_ref[...].astype(F32)
    stage[pl.ds(0, 10), pl.ds(1280, 640)] = wkv_ref[...].astype(F32)
    stage[pl.ds(0, 10), pl.ds(1920, 1280)] = wo_ref[...].astype(F32)
    lane = lax.broadcasted_iota(jnp.int32, (16, 256), 1)
    for g in range(GROUP):
        k, half = g // 2, g % 2
        start = 160 * g
        base = start // 128 * 128
        q = stage[:, base : base + 256]
        if start > base:
            q = pltpu.roll(q, 256 - (start - base), 1)
        start = 320 * half + HEAD_DIM * k
        base = min(start // 128 * 128, 384)
        rest_ = stage[:, 1280 + base : 1536 + base]
        shift = (160 - (start - base)) % 256
        if shift:
            rest_ = pltpu.roll(rest_, shift, 1)
        both = jnp.where(lane < 160, q, jnp.where(lane < 240, rest_, 0.0)).astype(BF16)
        wp[g, 0] = both[:, :128]
        wp[g, 1] = both[:, 128:]
        for t in range(5):
            at = 1920 + 640 * half + 128 * t
            wp[g, 2 + t] = stage[:, at : at + 128].astype(BF16)
    for slot in range(DP):
        cache[slot] = cache_ref[slots[slot]]
    pl.semaphore_wait(barrier, GROUP - 1 + DP - 1)

    started = []

    def rcopy(src, dst, sem, dev):
        cp = pltpu.make_async_remote_copy(
            src_ref=src,
            dst_ref=dst,
            send_sem=send.at[sem],
            recv_sem=recv.at[sem],
            device_id=dev,
            device_id_type=MESH,
        )
        cp.start()
        started.append(cp)
        return cp

    nlocal = [0]

    def lcopy(src, dst):
        cp = pltpu.make_async_copy(src, dst, local.at[nlocal[0]])
        nlocal[0] += 1
        cp.start()
        return cp

    twin = (dp, zh * 2 + 1 - c)

    s1 = []
    for d in range(1, GROUP):
        g = (f + d) % GROUP
        s1.append(
            rcopy(
                wp.at[g, :, pl.ds(0, S1ROWS), :],
                s1buf.at[:, pl.ds(pl.multiple_of(f * 16, 16), S1ROWS), :],
                S1 + d,
                (dp, g),
            )
        )
    zp, zm = (zh + 1) % NZH, (zh + NZH - 1) % NZH
    zo = (zh + 2) % NZH
    def page_copy(d):
        there = (dp + d) % DP
        return pltpu.make_async_remote_copy(
            src_ref=cache.at[there],
            dst_ref=cbuf.at[dp],
            send_sem=send.at[C1 + d],
            recv_sem=recv.at[C1 + d],
            device_id=(there, f),
            device_id_type=MESH,
        )

    def page_start(d, carry):
        page_copy(d).start()
        return carry

    lax.fori_loop(1, DP, page_start, 0)
    t0 = rcopy(tok, toks_all.at[f], TK + 0, (dp, zp * 2 + c))
    t1 = rcopy(tok, toks_all.at[f], TK + 1, (dp, zm * 2 + c))
    t4 = rcopy(tok, toks_all.at[f], TK + 4, twin)
    tl = lcopy(tok, toks_all.at[f])
    cbuf[dp] = cache[dp]

    length = lengths[slots[dp]]
    length_ref[...] = jnp.full((8, 128), length, jnp.int32)
    feature = lax.broadcasted_iota(jnp.int32, (TOK, 128), 1) % (HEAD_DIM // 2)
    frequency = jnp.zeros((TOK, 128), F32)
    for i in range(HEAD_DIM // 2):
        value = np.float32(ROPE_BASE) ** np.float32(-2.0 * i / HEAD_DIM)
        frequency = jnp.where(feature == i, float(value), frequency)

    def table(i, carry):
        position = length + i * TOK + lax.broadcasted_iota(jnp.int32, (TOK, 128), 0)
        angles = position.astype(F32) * frequency
        rows = pl.ds(pl.multiple_of(i * TOK, TOK), TOK)
        cos_ref[rows, :] = jnp.cos(angles)
        sin_ref[rows, :] = jnp.sin(angles)
        return carry

    s1buf[:, pl.ds(pl.multiple_of(f * 16, 16), 16), :] = wp[f]
    for cp in s1:
        cp.wait_recv()
    squeeze = one_hot(ROWS, 128, lambda r, l: l == 16 * (r // 10) + r % 10)
    for t in range(7):
        blk[t] = exact_dot(squeeze, s1buf[t]).astype(BF16)

    there = dp_of(y, 1 - zl, x)
    mine_q = w_qkv.at[c, :, y, zl, x]
    mine_o = w_out.at[c, :, y, zl, x]
    q2 = rcopy(blk.at[pl.ds(0, 2)], mine_q, S2 + 0, (there, f))
    lq = lcopy(blk.at[pl.ds(0, 2)], mine_q)
    o2 = rcopy(blk.at[pl.ds(2, 5)], mine_o, S2 + 1, (there, f))
    lo = lcopy(blk.at[pl.ds(2, 5)], mine_o)

    xp, xm, xo = (x + 1) % NX, (x + NX - 1) % NX, (x + 2) % NX
    yp, ym, yo = (y + 1) % NY, (y + NY - 1) % NY, (y + 2) % NY
    devices = {
        0: ((dp_of(y, zl, xp), f), (dp_of(y, zl, xm), f)),
        1: ((dp_of(yp, zl, x), f), (dp_of(ym, zl, x), f)),
    }
    along = {0: (x, xm, xp, xo), 1: (y, ym, yp, yo)}

    def near(unit, at, half=None):
        which, lo_, n, axis = unit
        arr = (w_qkv, w_out)[which]
        z = slice(None) if half is None else half
        if axis == 0:
            return arr.at[c, pl.ds(lo_, n), y, z, at]
        return arr.at[c, pl.ds(lo_, n), at, z, x]

    def far(unit, at, half=None):
        which, lo_, n, axis = unit
        arr = (w_qkv, w_out)[which]
        z = slice(None) if half is None else half
        if axis == 0:
            return arr.at[c, pl.ds(lo_, n), at, z]
        return arr.at[c, pl.ds(lo_, n), :, z, at]

    class Ring:
        def __init__(self, u, second):
            self.unit = UNITS[u]
            self.base = RING + PER_UNIT * u + (4 if second else 0)
            self.axis = self.unit[3] if not second else 1 - self.unit[3]
            self.part = far if second else near
            self.at, self.minus, self.plus, self.other = along[self.axis]

        def start(self):
            up, down = devices[self.axis]
            own = self.part(self.unit, self.at)
            self.a = rcopy(own, own, self.base + 0, up)
            self.b = rcopy(own, own, self.base + 1, down)

        def relay(self):
            up, down = devices[self.axis]
            self.a.wait_recv()
            piece = self.part(self.unit, self.minus, 0)
            self.c = rcopy(piece, piece, self.base + 2, up)
            self.b.wait_recv()
            piece = self.part(self.unit, self.plus, 1)
            self.d = rcopy(piece, piece, self.base + 3, down)

        def finish(self):
            self.c.wait_recv()
            self.d.wait_recv()

    firsts = [Ring(u, False) for u in range(4)]
    seconds = [Ring(u, True) for u in range(4)]
    hands = []

    def hand(u, k, ref):
        hands.append(rcopy(ref, ref, RING + PER_UNIT * u + 8 + k, twin))

    def hand_own(u):
        hand(u, 0, far(UNITS[u], seconds[u].at))

    def hand_next(u):
        s = seconds[u]
        hand(u, 1, far(UNITS[u], s.minus))
        hand(u, 2, far(UNITS[u], s.plus))

    def hand_last(u):
        s = seconds[u]
        hand(u, 3, far(UNITS[u], s.other, 0))
        hand(u, 4, far(UNITS[u], s.other, 1))

    q2.wait_recv()
    lq.wait()
    firsts[0].start()
    firsts[1].start()
    o2.wait_recv()
    lo.wait()
    firsts[2].start()
    firsts[3].start()
    firsts[0].relay()
    firsts[1].relay()
    for u in (0, 1):
        firsts[u].finish()
        seconds[u].start()
        hand_own(u)
    firsts[2].relay()
    firsts[3].relay()
    for u in (2, 3):
        firsts[u].finish()
        seconds[u].start()
        hand_own(u)

    lax.fori_loop(0, GROUP, table, 0)

    def page_wait(d, carry):
        page_copy(d).wait_recv()
        return carry

    lax.fori_loop(1, DP, page_wait, 0)
    pages = cbuf[...].reshape(DP * PAGE, 2 * KV_HEADS * HEAD_DIM)
    for k in range(KV_HEADS):

        def pick(r, l, k=k):
            value = KV_HEADS * HEAD_DIM + HEAD_DIM * k
            key = (l < 80) & (r == HEAD_DIM * k + l)
            front = (l >= 80) & (l < 128) & (r == value + l - 80)
            back = (l >= 128) & (r == value + 48 + l % 32)
            return key | front | back

        both = exact_dot(pages, one_hot(640, 256, pick))
        pack[k, pl.ds(0, 512), :] = both[:, :128].astype(BF16)
        lane = lax.broadcasted_iota(jnp.int32, (128, 128), 1) // 32
        tail = jnp.zeros((128, 128), F32)
        for g in range(4):
            tail = jnp.where(lane == g, both[128 * g : 128 * g + 128, 128:], tail)
        pack[k, pl.ds(512, 128), :] = tail.astype(BF16)
    up, down = (dp, zp * 2 + c), (dp, zm * 2 + c)
    h0 = rcopy(pack.at[zp], kv.at[c, zh], CX + 0, up)
    h1 = rcopy(pack.at[zm], kv.at[c, zh], CX + 1, down)
    h2 = rcopy(pack.at[zo, pl.ds(0, 320)], relay.at[0], CX + 2, up)
    h3 = rcopy(pack.at[zo, pl.ds(320, 320)], relay.at[1], CX + 3, down)
    hl = lcopy(pack.at[zh], kv.at[c, zh])
    hands.append(rcopy(pack.at[zh], kv.at[c, zh], CX + 6, twin))

    for u in (0, 1):
        seconds[u].relay()
        hand_next(u)
    t0.wait_recv()
    ref = toks_all.at[zm * 2 + c]
    t2 = rcopy(
        toks_all.at[zm * 2 + c, pl.ds(0, 32)],
        toks_all.at[zm * 2 + c, pl.ds(0, 32)],
        TK + 2,
        (dp, zp * 2 + c),
    )
    t5 = rcopy(ref, ref, TK + 5, twin)
    t1.wait_recv()
    ref = toks_all.at[zp * 2 + c]
    t3 = rcopy(
        toks_all.at[zp * 2 + c, pl.ds(32, 32)],
        toks_all.at[zp * 2 + c, pl.ds(32, 32)],
        TK + 3,
        (dp, zm * 2 + c),
    )
    t6 = rcopy(ref, ref, TK + 6, twin)
    h2.wait_recv()
    h4 = rcopy(relay.at[0], kv.at[c, zm, pl.ds(0, 320)], CX + 4, up)
    h3.wait_recv()
    h5 = rcopy(relay.at[1], kv.at[c, zp, pl.ds(320, 320)], CX + 5, down)
    for u in (2, 3):
        seconds[u].relay()
        hand_next(u)
    t2.wait_recv()
    ref = toks_all.at[zo * 2 + c, pl.ds(0, 32)]
    t7 = rcopy(ref, ref, TK + 7, twin)
    t3.wait_recv()
    ref = toks_all.at[zo * 2 + c, pl.ds(32, 32)]
    t8 = rcopy(ref, ref, TK + 8, twin)
    for u in (0, 1):
        seconds[u].finish()
        hand_last(u)
    h0.wait_recv()
    ref = kv.at[c, zm]
    hands.append(rcopy(ref, ref, CX + 7, twin))
    h1.wait_recv()
    ref = kv.at[c, zp]
    hands.append(rcopy(ref, ref, CX + 8, twin))
    h4.wait_recv()
    ref = kv.at[c, zo, pl.ds(0, 320)]
    hands.append(rcopy(ref, ref, CX + 9, twin))
    h5.wait_recv()
    ref = kv.at[c, zo, pl.ds(320, 320)]
    hands.append(rcopy(ref, ref, CX + 10, twin))
    for u in (2, 3):
        seconds[u].finish()
        hand_last(u)

    for cp in (t4, t5, t6, t7, t8, *hands):
        cp.wait_recv()
    for cp in started:
        cp.wait_send()

    def page_sent(d, carry):
        page_copy(d).wait_send()
        return carry

    lax.fori_loop(1, DP, page_sent, 0)
    tl.wait()
    hl.wait()


def gather_all(slots, lengths, raw, gain, w_query, w_keyval, w_out, cache):
    vmem = pl.BlockSpec(memory_space=pltpu.VMEM)
    hbm = pl.BlockSpec(memory_space=pl.ANY)
    far = pl.BlockSpec(memory_space=pltpu.HBM)
    return pl.pallas_call(
        gather_kernel,
        out_shape=(
            jax.ShapeDtypeStruct((GROUP, TOK, WIDTH), BF16),
            jax.ShapeDtypeStruct((2, 2, NY, NZL, NX, ROWS, 128), BF16),
            jax.ShapeDtypeStruct((2, 5, NY, NZL, NX, ROWS, 128), BF16),
            jax.ShapeDtypeStruct((2, NZH, 640, 128), BF16),
            jax.ShapeDtypeStruct((GROUP * TOK, 128), F32),
            jax.ShapeDtypeStruct((GROUP * TOK, 128), F32),
            jax.ShapeDtypeStruct((8, 128), jnp.int32),
        ),
        in_specs=[pl.BlockSpec(memory_space=pltpu.SMEM)] * 2 + [far, vmem] + [far] * 4,
        out_specs=(hbm, hbm, hbm, hbm, vmem, vmem, vmem),
        scratch_shapes=[
            pltpu.VMEM((TOK, WIDTH), BF16),
            pltpu.VMEM((10, 1280), BF16),
            pltpu.VMEM((10, 640), BF16),
            pltpu.VMEM((10, 1280), BF16),
            pltpu.VMEM((DP, PAGE, 640), BF16),
            pltpu.SemaphoreType.DMA((5,)),
            pltpu.VMEM((TOK, WIDTH), BF16),
            pltpu.VMEM((16, 3200), F32),
            pltpu.VMEM((GROUP, 7, 16, 128), BF16),
            pltpu.VMEM((DP, PAGE, 640), BF16),
            pltpu.VMEM((7, 128, 128), BF16),
            pltpu.VMEM((7, ROWS, 128), BF16),
            pltpu.VMEM((DP, PAGE, 640), BF16),
            pltpu.VMEM((KV_HEADS, 640, 128), BF16),
            pltpu.VMEM((2, 320, 128), BF16),
            pltpu.SemaphoreType.DMA((NSEM,)),
            pltpu.SemaphoreType.DMA((NSEM,)),
            pltpu.SemaphoreType.DMA((8,)),
        ],
        compiler_params=pltpu.CompilerParams(
            collective_id=0, has_side_effects=True, vmem_limit_bytes=40 * 1024 * 1024
        ),
        name="gather_all",
    )(slots, lengths, raw, gain, w_query, w_keyval, w_out, cache)


def attend_kernel(
    length_ref, x_ref, w_ref, kv_ref, cos_ref, sin_ref, out_ref, roped, kmat, vmat, qmat
):
    c, length = lax.axis_index("fsdp") % 2, length_ref[0:1, :]
    x = x_ref[...].reshape(GROUP * TOK, WIDTH)
    lane = lax.broadcasted_iota(jnp.int32, (GROUP * TOK, 256), 1)
    early = lane % HEAD_DIM < HEAD_DIM // 2
    narrow = cos_ref[...]
    cosine = jnp.concatenate([narrow, pltpu.roll(narrow, 120, 1)], axis=1)
    narrow = sin_ref[...]
    sine = jnp.concatenate([narrow, pltpu.roll(narrow, 120, 1)], axis=1)
    sine = jnp.where(early, -sine, sine)
    for half in range(2):
        w = jnp.concatenate([w_ref[half, 0], w_ref[half, 1]], axis=1)
        raw = exact_dot(x, w)
        turned = jnp.where(early, pltpu.roll(raw, 216, 1), pltpu.roll(raw, 40, 1))
        new = raw * cosine + turned * sine
        if half == 1:
            new = jnp.where(lane < 160, new, raw)
        roped[half] = new.astype(BF16).reshape(NZH, 2, TOK, 256)
    row = lax.broadcasted_iota(jnp.int32, (512, 128), 0)
    lane = lax.broadcasted_iota(jnp.int32, (512, 128), 1)
    for cs in range(2):
        for zs in range(NZH):
            base = (cs * NZH + zs) * 512
            a = kv_ref[cs, zs, pl.ds(0, 512), :]
            position = (row // 16) * 128 + zs * 32 + cs * 16 + row % 16
            bias = jnp.where((lane == 80) & (position >= length), NEGATIVE, 0.0)
            kmat[pl.ds(base, 512), :] = jnp.where(lane < 80, a.astype(F32), bias).astype(BF16)
            vmat[pl.ds(base, 512), pl.ds(0, 128)] = a
            tail = kv_ref[cs, zs, pl.ds(512, 128), :]
            ones = jnp.where(lane[:128] == 32, 1.0, 0.0)
            for g in range(4):
                pick = one_hot(128, 128, lambda r, l: (l < 32) & (r == 32 * g + l))
                vmat[pl.ds(base + 128 * g, 128), pl.ds(128, 128)] = (
                    exact_dot(tail, pick) + ones
                ).astype(BF16)
    first = roped[0].reshape(512, 256)
    second = roped[1].reshape(512, 256)
    to_key = one_hot(256, 128, lambda r, l: (l < 80) & (r == 160 + l))
    kmat[pl.ds(4096, 512), :] = exact_dot(first, to_key).astype(BF16)
    to_value = one_hot(256, 256, lambda r, l: (l >= 80) & (l < 160) & (r == 80 + l))
    lane = lax.broadcasted_iota(jnp.int32, (512, 256), 1)
    ones = jnp.where(lane == 160, 1.0, 0.0)
    vmat[pl.ds(4096, 512), :] = (exact_dot(second, to_value) + ones).astype(BF16)

    lane = lax.broadcasted_iota(jnp.int32, (256, 128), 1)
    ones = jnp.where(lane == 80, 1.0, 0.0)
    own = [roped[half, :, c].reshape(256, 256) for half in range(2)]
    for h in range(4):
        off = HEAD_DIM * (h % 2)
        to_head = one_hot(256, 128, lambda r, l: (l < 80) & (r == off + l))
        qmat[h] = (exact_dot(own[h // 2], to_head) + ones).astype(BF16)

    row = lax.broadcasted_iota(jnp.int32, (256, 512), 0)
    col = lax.broadcasted_iota(jnp.int32, (256, 512), 1)
    token = (row // 64) * 128 + c * 64 + row % 64
    causal = jnp.where(col <= token, 0.0, NEGATIVE)
    scale = LOG2E * HEAD_DIM ** (-0.5)
    nt = (((1,), (1,)), ((), ()))

    out = exact_dot(
        own[0], one_hot(256, 512, lambda r, l: (l >= 320) & (l < 400) & (r == l - 160))
    ) + exact_dot(
        own[1], one_hot(256, 512, lambda r, l: (l >= 400) & (l < 480) & (r == l - 240))
    )
    for h in range(4):
        q = qmat[h]
        s = lax.dot_general(q, kmat[pl.ds(4096, 512), :], nt, preferred_element_type=F32) + causal
        top = jnp.max(s, axis=1, keepdims=True)
        p = jnp.exp2((s - top) * scale).astype(BF16)
        acc = exact_dot(p, vmat[pl.ds(4096, 512), :])
        for j in range(4):
            s = lax.dot_general(
                q, kmat[pl.ds(1024 * j, 1024), :], nt, preferred_element_type=F32
            )
            new_top = jnp.maximum(top, jnp.max(s, axis=1, keepdims=True))
            p = jnp.exp2((s - new_top) * scale).astype(BF16)
            acc = acc * jnp.exp2((top - new_top) * scale) + exact_dot(
                p, vmat[pl.ds(1024 * j, 1024), :]
            )
            top = new_top
        att = (acc / acc[:, 160:161]).astype(BF16)
        out = out + exact_dot(
            att,
            one_hot(256, 512, lambda r, l: (r >= 80) & (r < 160) & (l == 80 * h + r - 80)),
        )
    out_ref[...] = out.astype(BF16).reshape(NZH, TOK, 512)


def attend(length, x, w, kv, cosine, sine):
    vmem = pl.BlockSpec(memory_space=pltpu.VMEM)
    return pl.pallas_call(
        attend_kernel,
        out_shape=jax.ShapeDtypeStruct((NZH, TOK, 512), BF16),
        in_specs=[vmem] * 6,
        out_specs=vmem,
        scratch_shapes=[
            pltpu.VMEM((2, NZH, 2, TOK, 256), BF16),
            pltpu.VMEM((4608, 128), BF16),
            pltpu.VMEM((4608, 256), BF16),
            pltpu.VMEM((4, 256, 128), BF16),
        ],
        compiler_params=pltpu.CompilerParams(vmem_limit_bytes=30 * 1024 * 1024),
        name="attend",
    )(length, x, w, kv, cosine, sine)


def project_kernel(msg, w, upd_hbm, keyval_hbm, rbuf, upd_ref, keyval_ref, send, recv, local):
    dp = lax.axis_index("dp")
    f = lax.axis_index("fsdp")
    zh, c = f // 2, f % 2
    load = pltpu.make_async_copy(msg.at[zh], rbuf.at[zh], local.at[0])
    load.start()
    barrier = pltpu.get_barrier_semaphore()
    for d in range(1, NZH):
        g = (zh + d) % NZH
        pl.semaphore_signal(barrier, inc=1, device_id=(dp, g * 2 + c), device_id_type=MESH)
    pl.semaphore_wait(barrier, NZH - 1)
    copies = []
    for d in range(1, NZH):
        g = (zh + d) % NZH
        cp = pltpu.make_async_remote_copy(
            src_ref=msg.at[g],
            dst_ref=rbuf.at[zh],
            send_sem=send.at[d],
            recv_sem=recv.at[d],
            device_id=(dp, g * 2 + c),
            device_id_type=MESH,
        )
        cp.start()
        copies.append(cp)
    keyval = jnp.zeros((TOK, 640), F32)
    load.wait()
    for cp in copies:
        cp.wait_recv()
    lane = lax.broadcasted_iota(jnp.int32, (TOK, 128), 1)
    attended = []
    for pair in range(2):
        a = rbuf[2 * pair].astype(F32)
        b = pltpu.roll(rbuf[2 * pair + 1].astype(F32)[:, :384], 64, 1)
        attended += [
            a[:, 0:256],
            jnp.concatenate(
                [jnp.where(lane < 64, a[:, 256:384], b[:, 0:128]), b[:, 128:256]], axis=1
            ),
            b[:, 256:384],
        ]
    for k in range(KV_HEADS):

        def place(r, l, k=k):
            key = (r >= 64) & (r < 144) & (l == 80 * k + r - 64)
            value = (r >= 144) & (r < 224) & (l == 320 + 80 * k + r - 144)
            return key | value

        keyval = keyval + exact_dot(rbuf[k][:, 256:512], one_hot(256, 640, place))
    keyval_ref[...] = keyval.astype(BF16)
    stores = [pltpu.make_async_copy(keyval_ref, keyval_hbm, local.at[1])]
    stores[0].start()
    tiles = [t.astype(BF16) for t in attended]
    nt = (((1,), (1,)), ((), ()))
    spans = ((0, 2), (2, 2), (4, 1), (5, 2), (7, 2), (9, 1))
    for n in range(4):
        rows = pl.ds(640 * n, 640)
        total = jnp.zeros((TOK, 640), F32)
        for t, (lo, count) in zip(tiles, spans):
            parts = [w[(lo + i) // 5, (lo + i) % 5, rows, :] for i in range(count)]
            rhs = parts[0] if count == 1 else jnp.concatenate(parts, axis=1)
            total = total + lax.dot_general(t, rhs, nt, preferred_element_type=F32)
        upd_ref[:, 640 * n : 640 * n + 640] = total.astype(BF16)
        cols = pl.ds(640 * n, 640)
        cp = pltpu.make_async_copy(upd_ref.at[:, cols], upd_hbm.at[:, cols], local.at[2 + n])
        cp.start()
        stores.append(cp)
    for cp in copies:
        cp.wait_send()
    for cp in stores:
        cp.wait()


def project(msg, w):
    vmem = pl.BlockSpec(memory_space=pltpu.VMEM)
    far = pl.BlockSpec(memory_space=pltpu.HBM)
    return pl.pallas_call(
        project_kernel,
        out_shape=(
            jax.ShapeDtypeStruct((TOK, WIDTH), BF16),
            jax.ShapeDtypeStruct((TOK, 640), BF16),
        ),
        in_specs=[pl.BlockSpec(memory_space=pl.ANY), vmem],
        out_specs=(far, far),
        scratch_shapes=[
            pltpu.VMEM((NZH, TOK, 512), BF16),
            pltpu.VMEM((TOK, WIDTH), BF16),
            pltpu.VMEM((TOK, 640), BF16),
            pltpu.SemaphoreType.DMA((4,)),
            pltpu.SemaphoreType.DMA((4,)),
            pltpu.SemaphoreType.DMA((6,)),
        ],
        compiler_params=pltpu.CompilerParams(
            collective_id=1, has_side_effects=True, vmem_limit_bytes=20 * 1024 * 1024
        ),
        name="project",
    )(msg, w)


def on_device(
    stretch_tokens, norm_gain, w_query, w_keyval, w_out, cache_store, cache_lengths, source_slot
):
    toks_all, w_qkv, w_o, kv, cosine, sine, length = gather_all(
        source_slot,
        cache_lengths,
        stretch_tokens[0],
        norm_gain[None],
        w_query,
        w_keyval,
        w_out,
        cache_store,
    )
    qkv = w_qkv.reshape(2, 2, WIDTH, 128)
    msg = attend(length, toks_all, qkv, kv, cosine, sine)
    update, new_keyval = project(msg, w_o.reshape(2, 5, WIDTH, 128))
    return (update[None], new_keyval[None])


def solution(mesh):
    in_specs = (
        P("dp", "fsdp", None),
        P(),
        P(("dp", "fsdp"), None),
        P(("dp", "fsdp"), None),
        P(("dp", "fsdp"), None),
        P(None, ("dp", "fsdp"), None),
        P(),
        P(),
    )
    out_specs = (P("dp", "fsdp", None), P("dp", "fsdp", None))
    return jax.shard_map(
        on_device, mesh=mesh, in_specs=in_specs, out_specs=out_specs, check_vma=False
    )
```
